256 devices in a mesh: row: 32 (over z, x), col: 4 (over y), rep: 2 (over core).
Axes of the slice: x: 4, y: 4, z: 8, core: 2. Of those that a mesh axis runs over, the one named last changes fastest.
Arguments:
- amplitudes: bfloat16 [32768, 8192], P('row', ('rep', 'col')), may hold values from -6 to 6
- integrals: bfloat16 [8192, 4096], P(('rep', 'row'), 'col'), may hold values from -0.1875 to 0.1875
- tile_mask: int32 [64, 32], replicated, may hold values from 0 to 1
- k_irrep: int32 [64], replicated, may hold values from 0 to 3
- n_irrep: int32 [32], replicated, may hold values from 0 to 3
- stored_tile: int32 [64], replicated, may hold values from 0 to 63, as said below
Outputs:
- ladder: bfloat16 [32768, 4096], P('row', ('col', 'rep'))
The draws below stay inside these ranges and needn't reach their ends.
Inputs may be any that keep to these rules, and one draw needn't show every extreme that they name: `stored_tile`: for each q, slots q * 32 to (q + 1) * 32 - 1 hold a permutation of the tiles q * 32 to (q + 1) * 32 - 1.
All inputs are finite; a program needn't handle non-finite values.
Results may differ from the reference program's by a relative error of at most 0.001.
Values may be sent and summed in bfloat16 or wider, within the bound.
No kernel may reach another device: no remote copies, remote signals or barrier semaphores. Data moves between devices by JAX's collectives and lax.ppermute only.
A program may use at most 128 MiB of HBM per device.

```python
import jax
import jax.numpy as jnp

TS = 128
NCOL = 1024
M = 32768
K = 8192
N = 4096
KS = 32
KT = 64
NT = 32


def draw_stored_tile(key, part):
    scores = jax.random.randint(key, (KT,), 0, 1 << 20) * KT + jnp.arange(KT, dtype=jnp.int32)
    grouped = scores.reshape(KT // KS, KS)
    order = jnp.argsort(grouped, axis=1, stable=True).astype(jnp.int32)
    offsets = (jnp.arange(KT // KS, dtype=jnp.int32) * KS)[:, None]
    return (order + offsets).reshape(KT).astype(jnp.int32)


def dense_choice(key):
    seed_key = jax.random.fold_in(key, 7001)
    dense_slab = jax.random.randint(jax.random.fold_in(seed_key, 1), (), 0, KT // KS).astype(jnp.int32)
    dense_col = jax.random.randint(jax.random.fold_in(seed_key, 2), (), 0, NT // (NCOL // TS)).astype(jnp.int32)
    dense_label = jax.random.randint(jax.random.fold_in(seed_key, 3), (), 0, 4).astype(jnp.int32)
    return (dense_slab, dense_col, dense_label)


def slab_ids():
    return (jnp.arange(KT, dtype=jnp.int32) // KS).astype(jnp.int32)


def column_ids():
    return (jnp.arange(NT, dtype=jnp.int32) // (NCOL // TS)).astype(jnp.int32)


def draw_k_irrep(key, part):
    dense_slab, dense_col, dense_label = dense_choice(key)
    base_labels = jax.random.randint(jax.random.fold_in(key, 7101), (KT,), 0, 4).astype(jnp.int32)
    return jnp.where(slab_ids() == dense_slab, dense_label, base_labels).astype(jnp.int32)


def draw_n_irrep(key, part):
    dense_slab, dense_col, dense_label = dense_choice(key)
    base_labels = jax.random.randint(jax.random.fold_in(key, 7201), (NT,), 0, 4).astype(jnp.int32)
    return jnp.where(column_ids() == dense_col, dense_label, base_labels).astype(jnp.int32)


def draw_tile_mask(key, part):
    dense_slab, dense_col, dense_label = dense_choice(key)
    base_draw = jax.random.randint(jax.random.fold_in(key, 7301), (KT, NT), 0, 4)
    base_mask = (base_draw < 3).astype(jnp.int32)
    inside = jnp.logical_and((slab_ids() == dense_slab)[:, None], (column_ids() == dense_col)[None, :])
    return jnp.where(inside, 1, base_mask).astype(jnp.int32)


def strengthened(array, rng, source, target, blocks, factor):
    owner, partner = [(jnp.arange(array.shape[dim]) // (array.shape[dim] // blocks)).reshape([-1 if axis == dim else 1 for axis in range(array.ndim)]) for dim in (source, target)]
    chosen = jax.random.permutation(rng, blocks)[partner]
    strong = (owner == chosen) | (owner == (partner + blocks // 2) % blocks)
    return jnp.where(strong, factor * array, array)


def shard_levels(key, dims, shards, smallest, largest):
    def one(axis_at, parts):
        draws = jax.random.uniform(jax.random.fold_in(jax.random.fold_in(key, 6), axis_at), (parts,), jnp.float32, smallest / len(shards), largest / len(shards))
        return jnp.repeat(jnp.exp(draws), dims[axis_at] // parts).reshape((-1,) + (1,) * (len(dims) - axis_at - 1))

    level = one(*shards[0])
    for cut in shards[1:]:
        level = level * one(*cut)
    return level


def normal_values(rng, shape, deviation, bound, pieces=(), kind=jnp.bfloat16):
    values = jax.random.normal(rng, shape, jnp.float32) * deviation
    if len(pieces) > 0:
        values = shard_levels(rng, shape, pieces, -0.22, 0.18) * values
    return jnp.clip(values, min=-bound, max=bound).astype(kind)


def heavy_noise(own_key, shape, width, limit, pieces, heavy, kind=jnp.bfloat16):
    entries = width * jax.random.normal(own_key, shape, jnp.float32)
    if pieces:
        entries = entries * shard_levels(own_key, shape, pieces, -0.22, 0.18)
    return jnp.clip(strengthened(entries, jax.random.fold_in(own_key, 3), *heavy), -limit, limit).astype(kind)


def setup_inputs(seed: int = 0) -> dict:
    seeds = jax.random.split(jax.random.key(seed), 7)
    amplitudes = normal_values(seeds[0], (M, K), 1.0, 6.0, ((0, 32), (1, 8)))
    integrals = heavy_noise(seeds[1], (K, N), K ** -0.5, 0.1875, ((0, 64), (1, 4)), (0, 1, 64, 4.0))
    tile_mask = draw_tile_mask(jax.random.fold_in(seeds[6], 71), 0)
    k_irrep = draw_k_irrep(jax.random.fold_in(seeds[6], 71), 0)
    n_irrep = draw_n_irrep(jax.random.fold_in(seeds[6], 71), 0)
    stored_tile = draw_stored_tile(jax.random.fold_in(seeds[6], 71), 0)
    return {"amplitudes": amplitudes, "integrals": integrals, "tile_mask": tile_mask, "k_irrep": k_irrep, "n_irrep": n_irrep, "stored_tile": stored_tile}


def reference(amplitudes, integrals, tile_mask, k_irrep, n_irrep, stored_tile):
    allowed = jnp.logical_and(k_irrep[:, None] == n_irrep[None, :], tile_mask == 1)
    allowed_slots = jnp.take(allowed, stored_tile, axis=0).astype(jnp.bfloat16)
    blocks = integrals.reshape(KT, TS, NT, TS) * allowed_slots[:, None, :, None]
    ordered = jnp.take(amplitudes.reshape(M, KT, TS), stored_tile, axis=1).reshape(M, K)
    return jnp.dot(ordered, blocks.reshape(K, N), preferred_element_type=jnp.float32).astype(jnp.bfloat16)
```

```python
import jax
import jax.numpy as jnp
from jax import lax
from jax.sharding import PartitionSpec as P

TS = 128
X_RING = 4


def ring_perm(total, n, stride, step):
    pairs = []
    for i in range(total):
        base = (i // (stride * n)) * (stride * n) + i % stride
        pos = (i // stride) % n
        pairs.append((i, base + ((pos + step) % n) * stride))
    return pairs


def ring_gather(x, axis, total, n, stride):
    if n == 1:
        return [x]
    plus = ring_perm(total, n, stride, 1)
    minus = ring_perm(total, n, stride, -1)
    chunks = {0: x}
    if n == 2:
        chunks[1] = lax.ppermute(x, axis, plus)
        return [chunks[0], chunks[1]]
    cur_p, cur_m = x, x
    for k in range(1, (n - 1) // 2 + 1):
        cur_p = lax.ppermute(cur_p, axis, plus)
        cur_m = lax.ppermute(cur_m, axis, minus)
        chunks[(-k) % n] = cur_p
        chunks[k] = cur_m
    if n % 2 == 0:
        h = cur_p.shape[0] // 2
        first = lax.ppermute(cur_p[:h], axis, plus)
        second = lax.ppermute(cur_m[h:], axis, minus)
        chunks[n // 2] = jnp.concatenate([first, second], axis=0)
    return [chunks[d] for d in range(n)]


def on_device(amplitudes, integrals, tile_mask, k_irrep, n_irrep, stored_tile):
    slab = lax.axis_index("rep")
    column = lax.axis_index("col")
    row = lax.axis_index("row")
    n_row = lax.axis_size("row")
    n_col = lax.axis_size("col")
    nx = X_RING if n_row % X_RING == 0 else 1
    nz = n_row // nx
    zi = row // nx
    xi = row % nx

    ncol = integrals.shape[1]
    tiles_col = ncol // TS
    stored_rows = integrals.shape[0]
    slab_tiles = stored_rows * n_row // TS
    mrow = amplitudes.shape[0]
    chunk_tiles = amplitudes.shape[1] // TS

    n_labels = lax.dynamic_slice_in_dim(n_irrep, column * tiles_col, tiles_col)
    mask_cols = lax.dynamic_slice_in_dim(tile_mask, column * tiles_col, tiles_col, 1)
    slots = lax.dynamic_slice_in_dim(stored_tile, slab * slab_tiles, slab_tiles)
    same = jnp.take(k_irrep, slots)[:, None] == n_labels[None, :]
    occupied = jnp.take(mask_cols, slots, axis=0) == 1
    weights = jnp.logical_and(same, occupied).astype(jnp.bfloat16)
    local_ids = slots - slab * slab_tiles
    inverse = jnp.zeros((slab_tiles,), jnp.int32).at[local_ids].set(
        jnp.arange(slab_tiles, dtype=jnp.int32)
    )

    half = stored_rows // 2
    xs = ring_gather(integrals[:half], "row", n_row, nx, 1)
    zs = ring_gather(jnp.stack(xs), "row", n_row, nz, nx)
    g1 = jnp.stack(zs)
    zs2 = ring_gather(integrals[half:], "row", n_row, nz, nx)
    xs2 = ring_gather(jnp.stack(zs2), "row", n_row, nx, 1)
    g2 = jnp.swapaxes(jnp.stack(xs2), 0, 1)
    gathered = jnp.concatenate([g1, g2], axis=2).reshape(n_row, stored_rows, ncol)

    amp_chunks = ring_gather(amplitudes, "col", n_col, n_col, 1)

    partial_value = None
    for d in range(n_col):
        cprime = (column + d) % n_col
        tiles = cprime * chunk_tiles + jnp.arange(chunk_tiles, dtype=jnp.int32)
        slot_ids = jnp.take(inverse, tiles)
        sz = slot_ids // (stored_rows // TS) // nx
        sx = slot_ids // (stored_rows // TS) % nx
        sub = slot_ids % (stored_rows // TS)
        pos = ((sz - zi) % nz) * nx + (sx - xi) % nx
        blocks = gathered.reshape(n_row * (stored_rows // TS), TS, tiles_col, TS)
        picked = jnp.take(blocks, pos * (stored_rows // TS) + sub, axis=0)
        wsel = jnp.take(weights, slot_ids, axis=0)
        masked = (picked * wsel[:, None, :, None]).reshape(chunk_tiles * TS, ncol)
        term = jnp.dot(amp_chunks[d], masked, preferred_element_type=jnp.float32)
        partial_value = term if partial_value is None else partial_value + term

    n_rep = lax.axis_size("rep")
    width = ncol // n_rep
    if n_rep == 1:
        return partial_value.astype(jnp.bfloat16)
    parts = partial_value.reshape(mrow, n_rep, width)
    other = 1 - slab
    send = lax.dynamic_index_in_dim(parts, other, axis=1, keepdims=False)
    keep = lax.dynamic_index_in_dim(parts, slab, axis=1, keepdims=False)
    got = lax.ppermute(send, "rep", [(0, 1), (1, 0)])
    return (keep + got).astype(jnp.bfloat16)


def solution(mesh):
    placed = (P("row", ("rep", "col")), P(("rep", "row"), "col"), P(), P(), P(), P())
    return jax.shard_map(
        on_device, mesh=mesh, in_specs=placed, out_specs=P("row", ("col", "rep")), check_vma=False
    )
```

```python
import functools

import jax
import jax.numpy as jnp
from jax import lax
from jax.experimental import pallas as pl
from jax.experimental.pallas import tpu as pltpu
from jax.sharding import Mesh, PartitionSpec as P

TS = 128
X_RING = 4
GROUP = 4
TN = 256


def ring_perm(total, n, stride, step):
    pairs = []
    for i in range(total):
        base = (i // (stride * n)) * (stride * n) + i % stride
        pos = (i // stride) % n
        pairs.append((i, base + ((pos + step) % n) * stride))
    return pairs


def ring_gather(x, axis, total, n, stride):
    if n == 1:
        return [x]
    plus = ring_perm(total, n, stride, 1)
    minus = ring_perm(total, n, stride, -1)
    chunks = {0: x}
    if n == 2:
        chunks[1] = lax.ppermute(x, axis, plus)
        return [chunks[0], chunks[1]]
    cur_p, cur_m = x, x
    for k in range(1, (n - 1) // 2 + 1):
        cur_p = lax.ppermute(cur_p, axis, plus)
        cur_m = lax.ppermute(cur_m, axis, minus)
        chunks[(-k) % n] = cur_p
        chunks[k] = cur_m
    if n % 2 == 0:
        h = cur_p.shape[0] // 2
        first = lax.ppermute(cur_p[:h], axis, plus)
        second = lax.ppermute(cur_m[h:], axis, minus)
        chunks[n // 2] = jnp.concatenate([first, second], axis=0)
    return [chunks[d] for d in range(n)]


def ladder_kernel(n_chunks, chunk_tiles, tiles_col, tab_ref, w_ref, *refs):
    a_refs = refs[:n_chunks]
    m_ref = refs[n_chunks]
    o_ref = refs[n_chunks + 1]
    j = pl.program_id(0)
    tn = o_ref.shape[1]
    per = tn // TS
    col_tile = lax.broadcasted_iota(jnp.int32, (1, tn), 1) // TS
    groups_per_chunk = chunk_tiles // GROUP
    for g in range(n_chunks * groups_per_chunk):
        d = g // groups_per_chunk
        off = (g % groups_per_chunk) * GROUP * TS
        pieces = []
        for u in range(GROUP):
            s = tab_ref[g * GROUP + u]
            piece = m_ref[pl.ds(pl.multiple_of(s * TS, TS), TS), :]
            wv = jnp.zeros((1, tn), jnp.int32)
            for t in range(per):
                wv = jnp.where(col_tile == t, w_ref[s * tiles_col + j * per + t], wv)
            pieces.append(jnp.where(wv != 0, piece, jnp.zeros_like(piece)))
        mg = jnp.concatenate(pieces, axis=0)
        term = jnp.dot(a_refs[d][:, off:off + GROUP * TS], mg, preferred_element_type=jnp.float32)
        if g == 0:
            o_ref[...] = term
        else:
            o_ref[...] += term


def ladder_matmul(tab, wflat, amp_chunks, m_all, tiles_col):
    mrow, ck = amp_chunks[0].shape
    n_chunks = len(amp_chunks)
    kk, ncol = m_all.shape
    tn = min(TN, ncol)
    kernel = functools.partial(ladder_kernel, n_chunks, ck // TS, tiles_col)
    a_spec = pl.BlockSpec((mrow, ck), lambda j, t, w: (0, 0))
    return pl.pallas_call(
        kernel,
        out_shape=jax.ShapeDtypeStruct((mrow, ncol), jnp.float32),
        grid_spec=pltpu.PrefetchScalarGridSpec(
            num_scalar_prefetch=2,
            grid=(ncol // tn,),
            in_specs=[a_spec] * n_chunks + [pl.BlockSpec((kk, tn), lambda j, t, w: (0, j))],
            out_specs=pl.BlockSpec((mrow, tn), lambda j, t, w: (0, j)),
        ),
        compiler_params=pltpu.CompilerParams(
            dimension_semantics=("arbitrary",), vmem_limit_bytes=56 * 1024 * 1024
        ),
    )(tab, wflat, *amp_chunks, m_all)


def on_device(amplitudes, integrals, tile_mask, k_irrep, n_irrep, stored_tile):
    slab = lax.axis_index("rep")
    column = lax.axis_index("col")
    n_col = lax.axis_size("col")
    n_row = lax.axis_size("z") * lax.axis_size("x")

    ncol = integrals.shape[1]
    tiles_col = ncol // TS
    stored_rows = integrals.shape[0]
    slab_tiles = stored_rows * n_row // TS
    mrow = amplitudes.shape[0]
    chunk_tiles = amplitudes.shape[1] // TS

    n_labels = lax.dynamic_slice_in_dim(n_irrep, column * tiles_col, tiles_col)
    mask_cols = lax.dynamic_slice_in_dim(tile_mask, column * tiles_col, tiles_col, 1)
    slots = lax.dynamic_slice_in_dim(stored_tile, slab * slab_tiles, slab_tiles)
    same = jnp.take(k_irrep, slots)[:, None] == n_labels[None, :]
    occupied = jnp.take(mask_cols, slots, axis=0) == 1
    weights = jnp.logical_and(same, occupied).astype(jnp.int32)
    local_ids = slots - slab * slab_tiles
    inverse = jnp.zeros((slab_tiles,), jnp.int32).at[local_ids].set(
        jnp.arange(slab_tiles, dtype=jnp.int32)
    )
    q = jnp.arange(n_col * chunk_tiles, dtype=jnp.int32)
    tab = jnp.take(inverse, ((column + q // chunk_tiles) % n_col) * chunk_tiles + q % chunk_tiles)

    gx = lax.all_gather(integrals, "x", axis=0, tiled=True)
    m_all = lax.all_gather(gx, "z", axis=0, tiled=True)

    amp_chunks = ring_gather(amplitudes, "col", n_col, n_col, 1)

    partial_value = ladder_matmul(tab, weights.reshape(-1), amp_chunks, m_all, tiles_col)

    n_rep = lax.axis_size("rep")
    width = ncol // n_rep
    parts = partial_value.reshape(mrow, n_rep, width)
    send = lax.dynamic_index_in_dim(parts, 1 - slab, axis=1, keepdims=False)
    keep = lax.dynamic_index_in_dim(parts, slab, axis=1, keepdims=False)
    got = lax.ppermute(send, "rep", [(0, 1), (1, 0)])
    return (keep + got).astype(jnp.bfloat16)


def solution(mesh):
    nrow = mesh.shape["row"]
    nx = X_RING if nrow % X_RING == 0 else 1
    devices = mesh.devices.reshape(nrow // nx, nx, mesh.shape["col"], mesh.shape["rep"])
    fine = Mesh(devices, ("z", "x", "col", "rep"))
    rows = ("z", "x")
    placed = (P(rows, ("rep", "col")), P(("rep",) + rows, "col"), P(), P(), P(), P())
    return jax.shard_map(
        on_device, mesh=fine, in_specs=placed, out_specs=P(rows, ("col", "rep")), check_vma=False
    )
```

```python
import functools

import jax
import jax.numpy as jnp
from jax import lax
from jax.experimental import pallas as pl
from jax.experimental.pallas import tpu as pltpu
from jax.sharding import Mesh, PartitionSpec as P

TS = 128
X_RING = 4
GROUP = 4
TN = 256


def ring_perm(total, n, stride, step):
    pairs = []
    for i in range(total):
        base = (i // (stride * n)) * (stride * n) + i % stride
        pos = (i // stride) % n
        pairs.append((i, base + ((pos + step) % n) * stride))
    return pairs


def ring_gather(x, axis, total, n, stride):
    if n == 1:
        return [x]
    plus = ring_perm(total, n, stride, 1)
    minus = ring_perm(total, n, stride, -1)
    chunks = {0: x}
    if n == 2:
        chunks[1] = lax.ppermute(x, axis, plus)
        return [chunks[0], chunks[1]]
    cur_p, cur_m = x, x
    for k in range(1, (n - 1) // 2 + 1):
        cur_p = lax.ppermute(cur_p, axis, plus)
        cur_m = lax.ppermute(cur_m, axis, minus)
        chunks[(-k) % n] = cur_p
        chunks[k] = cur_m
    if n % 2 == 0:
        h = cur_p.shape[0] // 2
        first = lax.ppermute(cur_p[:h], axis, plus)
        second = lax.ppermute(cur_m[h:], axis, minus)
        chunks[n // 2] = jnp.concatenate([first, second], axis=0)
    return [chunks[d] for d in range(n)]


def ladder_kernel(n_chunks, chunk_tiles, tiles_col, bpw, hsel_ref, tab_ref, pos_ref, w_ref, *refs):
    a_refs = refs[:n_chunks]
    m1_ref, m2_ref, o_ref = refs[n_chunks:n_chunks + 3]
    j = pl.program_id(0)
    tn = o_ref.shape[1]
    per = tn // TS
    hr = m1_ref.shape[0] // tab_ref.shape[0]
    first_tile = (hsel_ref[0] * bpw + j) * per
    col_tile = lax.broadcasted_iota(jnp.int32, (1, tn), 1) // TS
    groups_per_chunk = chunk_tiles // GROUP
    for g in range(n_chunks * groups_per_chunk):
        d = g // groups_per_chunk
        off = (g % groups_per_chunk) * GROUP * TS
        pieces = []
        for u in range(GROUP):
            s = tab_ref[g * GROUP + u]
            ps = pos_ref[s]
            top = m1_ref[pl.ds(pl.multiple_of(s * hr, hr), hr), :]
            bottom = m2_ref[pl.ds(pl.multiple_of(ps * hr, hr), hr), :]
            piece = jnp.concatenate([top, bottom], axis=0)
            wv = jnp.zeros((1, tn), jnp.int32)
            for t in range(per):
                wv = jnp.where(col_tile == t, w_ref[s * tiles_col + first_tile + t], wv)
            pieces.append(jnp.where(wv != 0, piece, jnp.zeros_like(piece)))
        mg = jnp.concatenate(pieces, axis=0)
        term = jnp.dot(a_refs[d][:, off:off + GROUP * TS], mg, preferred_element_type=jnp.float32)
        if g == 0:
            o_ref[...] = term
        else:
            o_ref[...] += term


def ladder_matmul(hsel, tab, pos, wflat, amp_chunks, m1, m2, tiles_col, width):
    mrow, ck = amp_chunks[0].shape
    n_chunks = len(amp_chunks)
    kk, ncol = m1.shape
    tn = min(TN, width)
    bpw = width // tn
    kernel = functools.partial(ladder_kernel, n_chunks, ck // TS, tiles_col, bpw)
    a_spec = pl.BlockSpec((mrow, ck), lambda j, h, t, p, w: (0, 0))
    m_spec = pl.BlockSpec((kk, tn), lambda j, h, t, p, w: (0, h[0] * bpw + j))
    return pl.pallas_call(
        kernel,
        out_shape=jax.ShapeDtypeStruct((mrow, width), jnp.float32),
        grid_spec=pltpu.PrefetchScalarGridSpec(
            num_scalar_prefetch=4,
            grid=(bpw,),
            in_specs=[a_spec] * n_chunks + [m_spec, m_spec],
            out_specs=pl.BlockSpec((mrow, tn), lambda j, h, t, p, w: (0, j)),
        ),
        compiler_params=pltpu.CompilerParams(
            dimension_semantics=("arbitrary",), vmem_limit_bytes=56 * 1024 * 1024
        ),
    )(hsel, tab, pos, wflat, *amp_chunks, m1, m2)


def on_device(amplitudes, integrals, tile_mask, k_irrep, n_irrep, stored_tile):
    slab = lax.axis_index("rep")
    column = lax.axis_index("col")
    n_col = lax.axis_size("col")
    nz = lax.axis_size("z")
    nx = lax.axis_size("x")
    n_row = nz * nx
    zi = lax.axis_index("z")
    xi = lax.axis_index("x")

    ncol = integrals.shape[1]
    tiles_col = ncol // TS
    stored_rows = integrals.shape[0]
    slab_tiles = stored_rows * n_row // TS
    mrow = amplitudes.shape[0]
    chunk_tiles = amplitudes.shape[1] // TS

    n_labels = lax.dynamic_slice_in_dim(n_irrep, column * tiles_col, tiles_col)
    mask_cols = lax.dynamic_slice_in_dim(tile_mask, column * tiles_col, tiles_col, 1)
    slots = lax.dynamic_slice_in_dim(stored_tile, slab * slab_tiles, slab_tiles)
    same = jnp.take(k_irrep, slots)[:, None] == n_labels[None, :]
    occupied = jnp.take(mask_cols, slots, axis=0) == 1
    weights = jnp.logical_and(same, occupied).astype(jnp.int32)
    local_ids = slots - slab * slab_tiles
    inverse = jnp.zeros((slab_tiles,), jnp.int32).at[local_ids].set(
        jnp.arange(slab_tiles, dtype=jnp.int32)
    )
    q = jnp.arange(n_col * chunk_tiles, dtype=jnp.int32)
    tab = jnp.take(inverse, ((column + q // chunk_tiles) % n_col) * chunk_tiles + q % chunk_tiles)

    amp_chunks = ring_gather(amplitudes, "col", n_col, n_col, 1)

    assert stored_rows == TS
    hr = stored_rows // 2
    m1 = lax.all_gather(integrals[:hr], ("z", "x"), axis=0, tiled=True)
    zs = ring_gather(integrals[hr:], ("z", "x"), n_row, nz, nx)
    xs = ring_gather(jnp.stack(zs), ("z", "x"), n_row, nx, 1)
    m2 = jnp.stack(xs).reshape(n_row * hr, ncol)
    sl = jnp.arange(slab_tiles, dtype=jnp.int32)
    pos = ((sl % nx - xi) % nx) * nz + (sl // nx - zi) % nz

    n_rep = lax.axis_size("rep")
    width = ncol // n_rep
    wflat = weights.reshape(-1)
    other = (1 - slab).astype(jnp.int32).reshape(1)
    own = slab.astype(jnp.int32).reshape(1)
    send = ladder_matmul(other, tab, pos, wflat, amp_chunks, m1, m2, tiles_col, width)
    got = lax.ppermute(send, "rep", [(0, 1), (1, 0)])
    keep = ladder_matmul(own, tab, pos, wflat, amp_chunks, m1, m2, tiles_col, width)
    return (keep + got).astype(jnp.bfloat16)


def solution(mesh):
    nrow = mesh.shape["row"]
    nx = X_RING if nrow % X_RING == 0 else 1
    devices = mesh.devices.reshape(nrow // nx, nx, mesh.shape["col"], mesh.shape["rep"])
    fine = Mesh(devices, ("z", "x", "col", "rep"))
    rows = ("z", "x")
    placed = (P(rows, ("rep", "col")), P(("rep",) + rows, "col"), P(), P(), P(), P())
    return jax.shard_map(
        on_device, mesh=fine, in_specs=placed, out_specs=P(rows, ("col", "rep")), check_vma=False
    )
```

```python
import functools

import jax
import jax.numpy as jnp
from jax import lax
from jax.experimental import pallas as pl
from jax.experimental.pallas import tpu as pltpu
from jax.sharding import Mesh, PartitionSpec as P

TS = 128
X_RING = 4
GROUP = 8
TN = 256


def ring_perm(total, n, stride, step):
    pairs = []
    for i in range(total):
        base = (i // (stride * n)) * (stride * n) + i % stride
        pos = (i // stride) % n
        pairs.append((i, base + ((pos + step) % n) * stride))
    return pairs


def ring_gather(x, axis, total, n, stride):
    if n == 1:
        return [x]
    plus = ring_perm(total, n, stride, 1)
    minus = ring_perm(total, n, stride, -1)
    chunks = {0: x}
    if n == 2:
        chunks[1] = lax.ppermute(x, axis, plus)
        return [chunks[0], chunks[1]]
    cur_p, cur_m = x, x
    for k in range(1, (n - 1) // 2 + 1):
        cur_p = lax.ppermute(cur_p, axis, plus)
        cur_m = lax.ppermute(cur_m, axis, minus)
        chunks[(-k) % n] = cur_p
        chunks[k] = cur_m
    if n % 2 == 0:
        h = cur_p.shape[0] // 2
        first = lax.ppermute(cur_p[:h], axis, plus)
        second = lax.ppermute(cur_m[h:], axis, minus)
        chunks[n // 2] = jnp.concatenate([first, second], axis=0)
    return [chunks[d] for d in range(n)]


def ladder_kernel(n_chunks, chunk_tiles, tiles_col, bpw, hsel_ref, tab_ref, pos_ref, w_ref, *refs):
    a_refs = refs[:n_chunks]
    m1_ref, m2_ref, o_ref = refs[n_chunks:n_chunks + 3]
    j = pl.program_id(0)
    tn = o_ref.shape[1]
    per = tn // TS
    hr = m1_ref.shape[0] // tab_ref.shape[0]
    first_tile = (hsel_ref[0] * bpw + j) * per
    col_tile = lax.broadcasted_iota(jnp.int32, (1, tn), 1) // TS
    groups_per_chunk = chunk_tiles // GROUP
    for g in range(n_chunks * groups_per_chunk):
        d = g // groups_per_chunk
        off = (g % groups_per_chunk) * GROUP * TS
        pieces = []
        for u in range(GROUP):
            s = tab_ref[g * GROUP + u]
            p1 = pos_ref[s]
            ps = pos_ref[tab_ref.shape[0] + s]
            top = m1_ref[pl.ds(pl.multiple_of(p1 * hr, hr), hr), :]
            bottom = m2_ref[pl.ds(pl.multiple_of(ps * hr, hr), hr), :]
            piece = jnp.concatenate([top, bottom], axis=0)
            wv = jnp.zeros((1, tn), jnp.int32)
            for t in range(per):
                wv = jnp.where(col_tile == t, w_ref[s * tiles_col + first_tile + t], wv)
            pieces.append(jnp.where(wv != 0, piece, jnp.zeros_like(piece)))
        mg = jnp.concatenate(pieces, axis=0)
        term = jnp.dot(a_refs[d][:, off:off + GROUP * TS], mg, preferred_element_type=jnp.float32)
        if g == 0:
            o_ref[...] = term
        else:
            o_ref[...] += term


def ladder_matmul(hsel, tab, pos, wflat, amp_chunks, m1, m2, tiles_col, width):
    mrow, ck = amp_chunks[0].shape
    n_chunks = len(amp_chunks)
    kk, ncol = m1.shape
    tn = min(TN, width)
    bpw = width // tn
    kernel = functools.partial(ladder_kernel, n_chunks, ck // TS, tiles_col, bpw)
    a_spec = pl.BlockSpec((mrow, ck), lambda j, h, t, p, w: (0, 0))
    m_spec = pl.BlockSpec((kk, tn), lambda j, h, t, p, w: (0, h[0] * bpw + j))
    return pl.pallas_call(
        kernel,
        out_shape=jax.ShapeDtypeStruct((mrow, width), jnp.float32),
        grid_spec=pltpu.PrefetchScalarGridSpec(
            num_scalar_prefetch=4,
            grid=(bpw,),
            in_specs=[a_spec] * n_chunks + [m_spec, m_spec],
            out_specs=pl.BlockSpec((mrow, tn), lambda j, h, t, p, w: (0, j)),
        ),
        compiler_params=pltpu.CompilerParams(
            dimension_semantics=("arbitrary",), vmem_limit_bytes=56 * 1024 * 1024
        ),
    )(hsel, tab, pos, wflat, *amp_chunks, m1, m2)


def on_device(amplitudes, integrals, tile_mask, k_irrep, n_irrep, stored_tile):
    slab = lax.axis_index("rep")
    column = lax.axis_index("col")
    n_col = lax.axis_size("col")
    nz = lax.axis_size("z")
    nx = lax.axis_size("x")
    n_row = nz * nx
    zi = lax.axis_index("z")
    xi = lax.axis_index("x")

    ncol = integrals.shape[1]
    tiles_col = ncol // TS
    stored_rows = integrals.shape[0]
    slab_tiles = stored_rows * n_row // TS
    mrow = amplitudes.shape[0]
    chunk_tiles = amplitudes.shape[1] // TS

    n_labels = lax.dynamic_slice_in_dim(n_irrep, column * tiles_col, tiles_col)
    mask_cols = lax.dynamic_slice_in_dim(tile_mask, column * tiles_col, tiles_col, 1)
    slots = lax.dynamic_slice_in_dim(stored_tile, slab * slab_tiles, slab_tiles)
    same = jnp.take(k_irrep, slots)[:, None] == n_labels[None, :]
    occupied = jnp.take(mask_cols, slots, axis=0) == 1
    weights = jnp.logical_and(same, occupied).astype(jnp.int32)
    local_ids = slots - slab * slab_tiles
    inverse = jnp.zeros((slab_tiles,), jnp.int32).at[local_ids].set(
        jnp.arange(slab_tiles, dtype=jnp.int32)
    )
    q = jnp.arange(n_col * chunk_tiles, dtype=jnp.int32)
    tab = jnp.take(inverse, ((column + q // chunk_tiles) % n_col) * chunk_tiles + q % chunk_tiles)

    amp_chunks = ring_gather(amplitudes, "col", n_col, n_col, 1)

    assert stored_rows == TS
    hr = stored_rows // 2
    xs1 = ring_gather(integrals[:hr], ("z", "x"), n_row, nx, 1)
    zs1 = ring_gather(jnp.stack(xs1), ("z", "x"), n_row, nz, nx)
    m1 = jnp.stack(zs1).reshape(n_row * hr, ncol)
    zs2 = ring_gather(integrals[hr:], ("z", "x"), n_row, nz, nx)
    xs2 = ring_gather(jnp.stack(zs2), ("z", "x"), n_row, nx, 1)
    m2 = jnp.stack(xs2).reshape(n_row * hr, ncol)
    sl = jnp.arange(slab_tiles, dtype=jnp.int32)
    rdx = (sl % nx - xi) % nx
    rdz = (sl // nx - zi) % nz
    pos = jnp.concatenate([rdz * nx + rdx, rdx * nz + rdz])

    n_rep = lax.axis_size("rep")
    width = ncol // n_rep
    wflat = weights.reshape(-1)
    other = (1 - slab).astype(jnp.int32).reshape(1)
    own = slab.astype(jnp.int32).reshape(1)
    send = ladder_matmul(other, tab, pos, wflat, amp_chunks, m1, m2, tiles_col, width)
    got = lax.ppermute(send, "rep", [(0, 1), (1, 0)])
    keep = ladder_matmul(own, tab, pos, wflat, amp_chunks, m1, m2, tiles_col, width)
    return (keep + got).astype(jnp.bfloat16)


def solution(mesh):
    nrow = mesh.shape["row"]
    nx = X_RING if nrow % X_RING == 0 else 1
    devices = mesh.devices.reshape(nrow // nx, nx, mesh.shape["col"], mesh.shape["rep"])
    fine = Mesh(devices, ("z", "x", "col", "rep"))
    rows = ("z", "x")
    placed = (P(rows, ("rep", "col")), P(("rep",) + rows, "col"), P(), P(), P(), P())
    return jax.shard_map(
        on_device, mesh=fine, in_specs=placed, out_specs=P(rows, ("col", "rep")), check_vma=False
    )
```

```python
import functools

import jax
import jax.numpy as jnp
from jax import lax
from jax.experimental import pallas as pl
from jax.experimental.pallas import tpu as pltpu
from jax.sharding import Mesh, PartitionSpec as P

TS = 128
X_RING = 4
GROUP = 8
TN = 256


def ring_perm(total, n, stride, step):
    pairs = []
    for i in range(total):
        base = (i // (stride * n)) * (stride * n) + i % stride
        pos = (i // stride) % n
        pairs.append((i, base + ((pos + step) % n) * stride))
    return pairs


def ring_gather(x, axis, total, n, stride):
    if n == 1:
        return [x]
    plus = ring_perm(total, n, stride, 1)
    minus = ring_perm(total, n, stride, -1)
    chunks = {0: x}
    if n == 2:
        chunks[1] = lax.ppermute(x, axis, plus)
        return [chunks[0], chunks[1]]
    cur_p, cur_m = x, x
    for k in range(1, (n - 1) // 2 + 1):
        cur_p = lax.ppermute(cur_p, axis, plus)
        cur_m = lax.ppermute(cur_m, axis, minus)
        chunks[(-k) % n] = cur_p
        chunks[k] = cur_m
    if n % 2 == 0:
        h = cur_p.shape[0] // 2
        first = lax.ppermute(cur_p[:h], axis, plus)
        second = lax.ppermute(cur_m[h:], axis, minus)
        chunks[n // 2] = jnp.concatenate([first, second], axis=0)
    return [chunks[d] for d in range(n)]


def ladder_kernel(chunk_ids, chunk_tiles, tiles_col, has_init, base_ref, tab_ref, pos_ref, w_ref, *refs):
    n_chunks = len(chunk_ids)
    a_refs = refs[:n_chunks]
    m1_ref, m2_ref = refs[n_chunks:n_chunks + 2]
    o_ref = refs[-1]
    j = pl.program_id(0)
    tn = o_ref.shape[1]
    per = tn // TS
    n_slots = tab_ref.shape[0]
    hr = m1_ref.shape[0] // n_slots
    first_tile = (base_ref[0] + j) * per
    col_tile = lax.broadcasted_iota(jnp.int32, (1, tn), 1) // TS
    for k, d in enumerate(chunk_ids):
        pieces = []
        for u in range(chunk_tiles):
            s = tab_ref[d * chunk_tiles + u]
            p1 = pos_ref[s]
            p2 = pos_ref[n_slots + s]
            top = m1_ref[pl.ds(pl.multiple_of(p1 * hr, hr), hr), :]
            bottom = m2_ref[pl.ds(pl.multiple_of(p2 * hr, hr), hr), :]
            piece = jnp.concatenate([top, bottom], axis=0)
            wv = jnp.zeros((1, tn), jnp.int32)
            for t in range(per):
                wv = jnp.where(col_tile == t, w_ref[s * tiles_col + first_tile + t], wv)
            pieces.append(jnp.where(wv != 0, piece, jnp.zeros_like(piece)))
        mg = jnp.concatenate(pieces, axis=0)
        term = jnp.dot(a_refs[k][...], mg, preferred_element_type=jnp.float32)
        if k == 0:
            if has_init:
                o_ref[...] = refs[n_chunks + 2][...] + term
            else:
                o_ref[...] = term
        else:
            o_ref[...] += term


def ladder_matmul(base, tab, pos, wflat, amp_chunks, chunk_ids, m1, m2, tiles_col, width, init=None):
    mrow, ck = amp_chunks[0].shape
    kk, ncol = m1.shape
    tn = min(TN, width)
    kernel = functools.partial(ladder_kernel, tuple(chunk_ids), ck // TS, tiles_col, init is not None)
    a_spec = pl.BlockSpec((mrow, ck), lambda j, b, t, p, w: (0, 0))
    m_spec = pl.BlockSpec((kk, tn), lambda j, b, t, p, w: (0, b[0] + j))
    in_specs = [a_spec] * len(amp_chunks) + [m_spec, m_spec]
    args = list(amp_chunks) + [m1, m2]
    if init is not None:
        in_specs.append(pl.BlockSpec((mrow, tn), lambda j, b, t, p, w: (0, b[0] + j)))
        args.append(init)
    return pl.pallas_call(
        kernel,
        out_shape=jax.ShapeDtypeStruct((mrow, width), jnp.float32),
        grid_spec=pltpu.PrefetchScalarGridSpec(
            num_scalar_prefetch=4,
            grid=(width // tn,),
            in_specs=in_specs,
            out_specs=pl.BlockSpec((mrow, tn), lambda j, b, t, p, w: (0, j)),
        ),
        compiler_params=pltpu.CompilerParams(
            dimension_semantics=("arbitrary",), vmem_limit_bytes=56 * 1024 * 1024
        ),
    )(base, tab, pos, wflat, *args)


def on_device(amplitudes, integrals, tile_mask, k_irrep, n_irrep, stored_tile):
    slab = lax.axis_index("rep")
    column = lax.axis_index("col")
    n_col = lax.axis_size("col")
    nz = lax.axis_size("z")
    nx = lax.axis_size("x")
    n_row = nz * nx
    zi = lax.axis_index("z")
    xi = lax.axis_index("x")

    ncol = integrals.shape[1]
    tiles_col = ncol // TS
    stored_rows = integrals.shape[0]
    slab_tiles = stored_rows * n_row // TS
    mrow = amplitudes.shape[0]
    chunk_tiles = amplitudes.shape[1] // TS

    n_labels = lax.dynamic_slice_in_dim(n_irrep, column * tiles_col, tiles_col)
    mask_cols = lax.dynamic_slice_in_dim(tile_mask, column * tiles_col, tiles_col, 1)
    slots = lax.dynamic_slice_in_dim(stored_tile, slab * slab_tiles, slab_tiles)
    same = jnp.take(k_irrep, slots)[:, None] == n_labels[None, :]
    occupied = jnp.take(mask_cols, slots, axis=0) == 1
    weights = jnp.logical_and(same, occupied).astype(jnp.int32)
    local_ids = slots - slab * slab_tiles
    inverse = jnp.zeros((slab_tiles,), jnp.int32).at[local_ids].set(
        jnp.arange(slab_tiles, dtype=jnp.int32)
    )
    q = jnp.arange(n_col * chunk_tiles, dtype=jnp.int32)
    tab = jnp.take(inverse, ((column + q // chunk_tiles) % n_col) * chunk_tiles + q % chunk_tiles)

    plus = ring_perm(n_col, n_col, 1, 1)
    minus = ring_perm(n_col, n_col, 1, -1)
    from_left = lax.ppermute(amplitudes, "col", plus)
    from_right = lax.ppermute(amplitudes, "col", minus)

    assert stored_rows == TS
    hr = stored_rows // 2
    xs1 = ring_gather(integrals[:hr], ("z", "x"), n_row, nx, 1)
    zs1 = ring_gather(jnp.stack(xs1), ("z", "x"), n_row, nz, nx)
    m1 = jnp.stack(zs1).reshape(n_row * hr, ncol)
    zs2 = ring_gather(integrals[hr:], ("z", "x"), n_row, nz, nx)
    bundle2, from_left, from_right = lax.optimization_barrier((jnp.stack(zs2), from_left, from_right))
    xs2 = ring_gather(bundle2, ("z", "x"), n_row, nx, 1)
    ha = mrow // 2
    far = jnp.concatenate(
        [lax.ppermute(from_left[:ha], "col", plus), lax.ppermute(from_right[ha:], "col", minus)], axis=0
    )
    m2 = jnp.stack(xs2).reshape(n_row * hr, ncol)
    sl = jnp.arange(slab_tiles, dtype=jnp.int32)
    rdx = (sl % nx - xi) % nx
    rdz = (sl // nx - zi) % nz
    pos = jnp.concatenate([rdz * nx + rdx, rdx * nz + rdz])

    n_rep = lax.axis_size("rep")
    width = ncol // n_rep
    wflat = weights.reshape(-1)
    zero = jnp.zeros((1,), jnp.int32)
    near = ladder_matmul(zero, tab, pos, wflat, [amplitudes, from_right, from_left], [0, 1, n_col - 1],
                         m1, m2, tiles_col, ncol)
    bpw = width // min(TN, width)
    other = ((1 - slab) * bpw).astype(jnp.int32).reshape(1)
    own = (slab * bpw).astype(jnp.int32).reshape(1)
    send = ladder_matmul(other, tab, pos, wflat, [far], [n_col // 2], m1, m2, tiles_col, width, near)
    got = lax.ppermute(send, "rep", [(0, 1), (1, 0)])
    keep = ladder_matmul(own, tab, pos, wflat, [far], [n_col // 2], m1, m2, tiles_col, width, near)
    return (keep + got).astype(jnp.bfloat16)


def solution(mesh):
    nrow = mesh.shape["row"]
    nx = X_RING if nrow % X_RING == 0 else 1
    devices = mesh.devices.reshape(nrow // nx, nx, mesh.shape["col"], mesh.shape["rep"])
    fine = Mesh(devices, ("z", "x", "col", "rep"))
    rows = ("z", "x")
    placed = (P(rows, ("rep", "col")), P(("rep",) + rows, "col"), P(), P(), P(), P())
    return jax.shard_map(
        on_device, mesh=fine, in_specs=placed, out_specs=P(rows, ("col", "rep")), check_vma=False
    )
```

```python
import functools

import jax
import jax.numpy as jnp
from jax import lax
from jax.experimental import pallas as pl
from jax.experimental.pallas import tpu as pltpu
from jax.sharding import Mesh, PartitionSpec as P

TS = 128
X_RING = 4
GROUP = 8
TN = 256


def ring_perm(total, n, stride, step):
    pairs = []
    for i in range(total):
        base = (i // (stride * n)) * (stride * n) + i % stride
        pos = (i // stride) % n
        pairs.append((i, base + ((pos + step) % n) * stride))
    return pairs


class Ring:
    def __init__(self, x, axis, total, n, stride):
        self.axis, self.n = axis, n
        self.plus = ring_perm(total, n, stride, 1)
        self.minus = ring_perm(total, n, stride, -1)
        self.chunks = {0: x}
        self.cur_p, self.cur_m = x, x
        self.k = 0
        self.steps = 0 if n == 1 else (n - 1) // 2 + (1 if n % 2 == 0 else 0)

    def step(self):
        self.k += 1
        k, n = self.k, self.n
        if n == 2:
            self.chunks[1] = lax.ppermute(self.cur_p, self.axis, self.plus)
        elif k <= (n - 1) // 2:
            self.cur_p = lax.ppermute(self.cur_p, self.axis, self.plus)
            self.cur_m = lax.ppermute(self.cur_m, self.axis, self.minus)
            self.chunks[(-k) % n] = self.cur_p
            self.chunks[k] = self.cur_m
        else:
            h = self.cur_p.shape[0] // 2
            first = lax.ppermute(self.cur_p[:h], self.axis, self.plus)
            second = lax.ppermute(self.cur_m[h:], self.axis, self.minus)
            self.chunks[n // 2] = jnp.concatenate([first, second], axis=0)

    def result(self):
        return jnp.stack([self.chunks[d] for d in range(self.n)])


def ladder_kernel(chunk_ids, chunk_tiles, tiles_col, has_init, base_ref, tab_ref, pos_ref, w_ref, *refs):
    n_chunks = len(chunk_ids)
    a_refs = refs[:n_chunks]
    m1_ref, m2_ref = refs[n_chunks:n_chunks + 2]
    o_ref = refs[-1]
    j = pl.program_id(0)
    tn = o_ref.shape[1]
    per = tn // TS
    n_slots = tab_ref.shape[0]
    hr = m1_ref.shape[0] // n_slots
    first_tile = (base_ref[0] + j) * per
    col_tile = lax.broadcasted_iota(jnp.int32, (1, tn), 1) // TS
    for k, d in enumerate(chunk_ids):
        pieces = []
        for u in range(chunk_tiles):
            s = tab_ref[d * chunk_tiles + u]
            p1 = pos_ref[s]
            p2 = pos_ref[n_slots + s]
            top = m1_ref[pl.ds(pl.multiple_of(p1 * hr, hr), hr), :]
            bottom = m2_ref[pl.ds(pl.multiple_of(p2 * hr, hr), hr), :]
            piece = jnp.concatenate([top, bottom], axis=0)
            wv = jnp.zeros((1, tn), jnp.int32)
            for t in range(per):
                wv = jnp.where(col_tile == t, w_ref[s * tiles_col + first_tile + t], wv)
            pieces.append(jnp.where(wv != 0, piece, jnp.zeros_like(piece)))
        mg = jnp.concatenate(pieces, axis=0)
        term = jnp.dot(a_refs[k][...], mg, preferred_element_type=jnp.float32)
        if k == 0:
            if has_init:
                o_ref[...] = refs[n_chunks + 2][...] + term
            else:
                o_ref[...] = term
        else:
            o_ref[...] += term


def ladder_matmul(base, tab, pos, wflat, amp_chunks, chunk_ids, m1, m2, tiles_col, width, init=None):
    mrow, ck = amp_chunks[0].shape
    kk, ncol = m1.shape
    tn = min(TN, width)
    kernel = functools.partial(ladder_kernel, tuple(chunk_ids), ck // TS, tiles_col, init is not None)
    a_spec = pl.BlockSpec((mrow, ck), lambda j, b, t, p, w: (0, 0))
    m_spec = pl.BlockSpec((kk, tn), lambda j, b, t, p, w: (0, b[0] + j))
    in_specs = [a_spec] * len(amp_chunks) + [m_spec, m_spec]
    args = list(amp_chunks) + [m1, m2]
    if init is not None:
        in_specs.append(pl.BlockSpec((mrow, tn), lambda j, b, t, p, w: (0, b[0] + j)))
        args.append(init)
    return pl.pallas_call(
        kernel,
        out_shape=jax.ShapeDtypeStruct((mrow, width), jnp.float32),
        grid_spec=pltpu.PrefetchScalarGridSpec(
            num_scalar_prefetch=4,
            grid=(width // tn,),
            in_specs=in_specs,
            out_specs=pl.BlockSpec((mrow, tn), lambda j, b, t, p, w: (0, j)),
        ),
        compiler_params=pltpu.CompilerParams(
            dimension_semantics=("arbitrary",), vmem_limit_bytes=56 * 1024 * 1024
        ),
    )(base, tab, pos, wflat, *args)


def on_device(amplitudes, integrals, tile_mask, k_irrep, n_irrep, stored_tile):
    slab = lax.axis_index("rep")
    column = lax.axis_index("col")
    n_col = lax.axis_size("col")
    nz = lax.axis_size("z")
    nx = lax.axis_size("x")
    n_row = nz * nx
    zi = lax.axis_index("z")
    xi = lax.axis_index("x")

    ncol = integrals.shape[1]
    tiles_col = ncol // TS
    stored_rows = integrals.shape[0]
    slab_tiles = stored_rows * n_row // TS
    mrow = amplitudes.shape[0]
    chunk_tiles = amplitudes.shape[1] // TS

    n_labels = lax.dynamic_slice_in_dim(n_irrep, column * tiles_col, tiles_col)
    mask_cols = lax.dynamic_slice_in_dim(tile_mask, column * tiles_col, tiles_col, 1)
    slots = lax.dynamic_slice_in_dim(stored_tile, slab * slab_tiles, slab_tiles)
    same = jnp.take(k_irrep, slots)[:, None] == n_labels[None, :]
    occupied = jnp.take(mask_cols, slots, axis=0) == 1
    weights = jnp.logical_and(same, occupied).astype(jnp.int32)
    local_ids = slots - slab * slab_tiles
    inverse = jnp.zeros((slab_tiles,), jnp.int32).at[local_ids].set(
        jnp.arange(slab_tiles, dtype=jnp.int32)
    )
    q = jnp.arange(n_col * chunk_tiles, dtype=jnp.int32)
    tab = jnp.take(inverse, ((column + q // chunk_tiles) % n_col) * chunk_tiles + q % chunk_tiles)

    plus = ring_perm(n_col, n_col, 1, 1)
    minus = ring_perm(n_col, n_col, 1, -1)
    from_left = lax.ppermute(amplitudes, "col", plus)
    from_right = lax.ppermute(amplitudes, "col", minus)

    assert stored_rows == TS
    hr = stored_rows // 2
    rows = ("z", "x")
    short1 = Ring(integrals[:hr], rows, n_row, nx, 1)
    short2 = Ring(integrals[hr:], rows, n_row, nz, nx)
    for _ in range(max(short1.steps, short2.steps)):
        if short1.k < short1.steps:
            short1.step()
        if short2.k < short2.steps:
            short2.step()
    bundle1, bundle2 = lax.optimization_barrier((short1.result(), short2.result()))
    long1 = Ring(bundle1, rows, n_row, nz, nx)
    long2 = Ring(bundle2, rows, n_row, nx, 1)
    tie_step = 2
    for i in range(max(long1.steps, long2.steps)):
        if long1.k < long1.steps:
            long1.step()
        if long2.k < long2.steps:
            long2.step()
        if i + 1 == tie_step:
            long1.cur_p, long1.cur_m, from_left, from_right = lax.optimization_barrier(
                (long1.cur_p, long1.cur_m, from_left, from_right)
            )
    m1 = long1.result().reshape(n_row * hr, ncol)
    ha = mrow // 2
    far = jnp.concatenate(
        [lax.ppermute(from_left[:ha], "col", plus), lax.ppermute(from_right[ha:], "col", minus)], axis=0
    )
    m2 = long2.result().reshape(n_row * hr, ncol)
    sl = jnp.arange(slab_tiles, dtype=jnp.int32)
    rdx = (sl % nx - xi) % nx
    rdz = (sl // nx - zi) % nz
    pos = jnp.concatenate([rdz * nx + rdx, rdx * nz + rdz])

    n_rep = lax.axis_size("rep")
    width = ncol // n_rep
    wflat = weights.reshape(-1)
    zero = jnp.zeros((1,), jnp.int32)
    near = ladder_matmul(zero, tab, pos, wflat, [amplitudes, from_right, from_left], [0, 1, n_col - 1],
                         m1, m2, tiles_col, ncol)
    bpw = width // min(TN, width)
    other = ((1 - slab) * bpw).astype(jnp.int32).reshape(1)
    own = (slab * bpw).astype(jnp.int32).reshape(1)
    send = ladder_matmul(other, tab, pos, wflat, [far], [n_col // 2], m1, m2, tiles_col, width, near)
    got = lax.ppermute(send, "rep", [(0, 1), (1, 0)])
    keep = ladder_matmul(own, tab, pos, wflat, [far], [n_col // 2], m1, m2, tiles_col, width, near)
    return (keep + got).astype(jnp.bfloat16)


def solution(mesh):
    nrow = mesh.shape["row"]
    nx = X_RING if nrow % X_RING == 0 else 1
    devices = mesh.devices.reshape(nrow // nx, nx, mesh.shape["col"], mesh.shape["rep"])
    fine = Mesh(devices, ("z", "x", "col", "rep"))
    rows = ("z", "x")
    placed = (P(rows, ("rep", "col")), P(("rep",) + rows, "col"), P(), P(), P(), P())
    return jax.shard_map(
        on_device, mesh=fine, in_specs=placed, out_specs=P(rows, ("col", "rep")), check_vma=False
    )
```

```python
import functools

import jax
import jax.numpy as jnp
from jax import lax
from jax.experimental import pallas as pl
from jax.experimental.pallas import tpu as pltpu
from jax.sharding import Mesh, PartitionSpec as P

TS = 128
X_RING = 4
GROUP = 8
TN = 256


def ring_perm(total, n, stride, step):
    pairs = []
    for i in range(total):
        base = (i // (stride * n)) * (stride * n) + i % stride
        pos = (i // stride) % n
        pairs.append((i, base + ((pos + step) % n) * stride))
    return pairs


class Ring:
    def __init__(self, x, axis, total, n, stride):
        self.axis, self.n = axis, n
        self.plus = ring_perm(total, n, stride, 1)
        self.minus = ring_perm(total, n, stride, -1)
        self.chunks = {0: x}
        self.cur_p, self.cur_m = x, x
        self.k = 0
        self.steps = 0 if n == 1 else (n - 1) // 2 + (1 if n % 2 == 0 else 0)

    def step(self):
        self.k += 1
        k, n = self.k, self.n
        if n == 2:
            self.chunks[1] = lax.ppermute(self.cur_p, self.axis, self.plus)
        elif k <= (n - 1) // 2:
            self.cur_p = lax.ppermute(self.cur_p, self.axis, self.plus)
            self.cur_m = lax.ppermute(self.cur_m, self.axis, self.minus)
            self.chunks[(-k) % n] = self.cur_p
            self.chunks[k] = self.cur_m
        else:
            h = self.cur_p.shape[0] // 2
            first = lax.ppermute(self.cur_p[:h], self.axis, self.plus)
            second = lax.ppermute(self.cur_m[h:], self.axis, self.minus)
            self.chunks[n // 2] = jnp.concatenate([first, second], axis=0)

    def result(self):
        return jnp.stack([self.chunks[d] for d in range(self.n)])


def direct_gather(x, axis, total, n, stride):
    chunks = {0: x}
    for d in range(1, (n + 1) // 2):
        chunks[d] = lax.ppermute(x, axis, ring_perm(total, n, stride, -d))
        chunks[n - d] = lax.ppermute(x, axis, ring_perm(total, n, stride, d))
    if n % 2 == 0 and n > 1:
        h = x.shape[0] // 2
        chunks[n // 2] = jnp.concatenate(
            [lax.ppermute(x[:h], axis, ring_perm(total, n, stride, n // 2)),
             lax.ppermute(x[h:], axis, ring_perm(total, n, stride, -(n // 2)))], axis=0)
    return jnp.stack([chunks[d] for d in range(n)])


def ladder_kernel(chunk_ids, chunk_tiles, tiles_col, has_init, base_ref, tab_ref, pos_ref, w_ref, *refs):
    n_chunks = len(chunk_ids)
    a_refs = refs[:n_chunks]
    m1_ref, m2_ref = refs[n_chunks:n_chunks + 2]
    o_ref = refs[-1]
    j = pl.program_id(0)
    tn = o_ref.shape[1]
    per = tn // TS
    n_slots = tab_ref.shape[0]
    hr = m1_ref.shape[0] // n_slots
    first_tile = (base_ref[0] + j) * per
    col_tile = lax.broadcasted_iota(jnp.int32, (1, tn), 1) // TS
    for k, d in enumerate(chunk_ids):
        pieces = []
        for u in range(chunk_tiles):
            s = tab_ref[d * chunk_tiles + u]
            p1 = pos_ref[s]
            p2 = pos_ref[n_slots + s]
            top = m1_ref[pl.ds(pl.multiple_of(p1 * hr, hr), hr), :]
            bottom = m2_ref[pl.ds(pl.multiple_of(p2 * hr, hr), hr), :]
            piece = jnp.concatenate([top, bottom], axis=0)
            wv = jnp.zeros((1, tn), jnp.int32)
            for t in range(per):
                wv = jnp.where(col_tile == t, w_ref[s * tiles_col + first_tile + t], wv)
            pieces.append(jnp.where(wv != 0, piece, jnp.zeros_like(piece)))
        mg = jnp.concatenate(pieces, axis=0)
        term = jnp.dot(a_refs[k][...], mg, preferred_element_type=jnp.float32)
        if k == 0:
            if has_init:
                o_ref[...] = refs[n_chunks + 2][...] + term
            else:
                o_ref[...] = term
        else:
            o_ref[...] += term


def ladder_matmul(base, tab, pos, wflat, amp_chunks, chunk_ids, m1, m2, tiles_col, width, init=None):
    mrow, ck = amp_chunks[0].shape
    kk, ncol = m1.shape
    tn = min(TN, width)
    kernel = functools.partial(ladder_kernel, tuple(chunk_ids), ck // TS, tiles_col, init is not None)
    a_spec = pl.BlockSpec((mrow, ck), lambda j, b, t, p, w: (0, 0))
    m_spec = pl.BlockSpec((kk, tn), lambda j, b, t, p, w: (0, b[0] + j))
    in_specs = [a_spec] * len(amp_chunks) + [m_spec, m_spec]
    args = list(amp_chunks) + [m1, m2]
    if init is not None:
        in_specs.append(pl.BlockSpec((mrow, tn), lambda j, b, t, p, w: (0, b[0] + j)))
        args.append(init)
    return pl.pallas_call(
        kernel,
        out_shape=jax.ShapeDtypeStruct((mrow, width), jnp.float32),
        grid_spec=pltpu.PrefetchScalarGridSpec(
            num_scalar_prefetch=4,
            grid=(width // tn,),
            in_specs=in_specs,
            out_specs=pl.BlockSpec((mrow, tn), lambda j, b, t, p, w: (0, j)),
        ),
        compiler_params=pltpu.CompilerParams(
            dimension_semantics=("arbitrary",), vmem_limit_bytes=56 * 1024 * 1024
        ),
    )(base, tab, pos, wflat, *args)


def on_device(amplitudes, integrals, tile_mask, k_irrep, n_irrep, stored_tile):
    slab = lax.axis_index("rep")
    column = lax.axis_index("col")
    n_col = lax.axis_size("col")
    nz = lax.axis_size("z")
    nx = lax.axis_size("x")
    n_row = nz * nx
    zi = lax.axis_index("z")
    xi = lax.axis_index("x")

    ncol = integrals.shape[1]
    tiles_col = ncol // TS
    stored_rows = integrals.shape[0]
    slab_tiles = stored_rows * n_row // TS
    mrow = amplitudes.shape[0]
    chunk_tiles = amplitudes.shape[1] // TS

    n_labels = lax.dynamic_slice_in_dim(n_irrep, column * tiles_col, tiles_col)
    mask_cols = lax.dynamic_slice_in_dim(tile_mask, column * tiles_col, tiles_col, 1)
    slots = lax.dynamic_slice_in_dim(stored_tile, slab * slab_tiles, slab_tiles)
    same = jnp.take(k_irrep, slots)[:, None] == n_labels[None, :]
    occupied = jnp.take(mask_cols, slots, axis=0) == 1
    weights = jnp.logical_and(same, occupied).astype(jnp.int32)
    local_ids = slots - slab * slab_tiles
    inverse = jnp.zeros((slab_tiles,), jnp.int32).at[local_ids].set(
        jnp.arange(slab_tiles, dtype=jnp.int32)
    )
    q = jnp.arange(n_col * chunk_tiles, dtype=jnp.int32)
    tab = jnp.take(inverse, ((column + q // chunk_tiles) % n_col) * chunk_tiles + q % chunk_tiles)

    plus = ring_perm(n_col, n_col, 1, 1)
    minus = ring_perm(n_col, n_col, 1, -1)
    from_left = lax.ppermute(amplitudes, "col", plus)
    from_right = lax.ppermute(amplitudes, "col", minus)

    assert stored_rows == TS
    hr = stored_rows // 2
    rows = ("z", "x")
    bundle1, bundle2 = lax.optimization_barrier(
        (direct_gather(integrals[:hr], rows, n_row, nx, 1), direct_gather(integrals[hr:], rows, n_row, nz, nx))
    )
    long1 = Ring(bundle1, rows, n_row, nz, nx)
    long2 = Ring(bundle2, rows, n_row, nx, 1)
    tie_step = 1
    for i in range(max(long1.steps, long2.steps)):
        if long1.k < long1.steps:
            long1.step()
        if long2.k < long2.steps:
            long2.step()
        if i + 1 == tie_step:
            long1.cur_p, long1.cur_m, from_left, from_right = lax.optimization_barrier(
                (long1.cur_p, long1.cur_m, from_left, from_right)
            )
    m1 = long1.result().reshape(n_row * hr, ncol)
    ha = mrow // 2
    far = jnp.concatenate(
        [lax.ppermute(from_left[:ha], "col", plus), lax.ppermute(from_right[ha:], "col", minus)], axis=0
    )
    m2 = long2.result().reshape(n_row * hr, ncol)
    sl = jnp.arange(slab_tiles, dtype=jnp.int32)
    rdx = (sl % nx - xi) % nx
    rdz = (sl // nx - zi) % nz
    pos = jnp.concatenate([rdz * nx + rdx, rdx * nz + rdz])

    n_rep = lax.axis_size("rep")
    width = ncol // n_rep
    wflat = weights.reshape(-1)
    bpw = width // min(TN, width)
    other = ((1 - slab) * bpw).astype(jnp.int32).reshape(1)
    own = (slab * bpw).astype(jnp.int32).reshape(1)
    chunks = [amplitudes, from_right, far, from_left]
    ids = list(range(n_col))
    send = ladder_matmul(other, tab, pos, wflat, chunks, ids, m1, m2, tiles_col, width)
    got = lax.ppermute(send, "rep", [(0, 1), (1, 0)])
    keep = ladder_matmul(own, tab, pos, wflat, chunks, ids, m1, m2, tiles_col, width)
    return (keep + got).astype(jnp.bfloat16)


def solution(mesh):
    nrow = mesh.shape["row"]
    nx = X_RING if nrow % X_RING == 0 else 1
    devices = mesh.devices.reshape(nrow // nx, nx, mesh.shape["col"], mesh.shape["rep"])
    fine = Mesh(devices, ("z", "x", "col", "rep"))
    rows = ("z", "x")
    placed = (P(rows, ("rep", "col")), P(("rep",) + rows, "col"), P(), P(), P(), P())
    return jax.shard_map(
        on_device, mesh=fine, in_specs=placed, out_specs=P(rows, ("col", "rep")), check_vma=False
    )
```

```python
import functools

import jax
import jax.numpy as jnp
from jax import lax
from jax.experimental import pallas as pl
from jax.experimental.pallas import tpu as pltpu
from jax.sharding import Mesh, PartitionSpec as P

TS = 128
X_RING = 4
GROUP = 4
TN = 256


def ring_perm(total, n, stride, step):
    pairs = []
    for i in range(total):
        base = (i // (stride * n)) * (stride * n) + i % stride
        pos = (i // stride) % n
        pairs.append((i, base + ((pos + step) % n) * stride))
    return pairs


def ring_gather(x, axis, total, n, stride):
    if n == 1:
        return [x]
    plus = ring_perm(total, n, stride, 1)
    minus = ring_perm(total, n, stride, -1)
    chunks = {0: x}
    if n == 2:
        chunks[1] = lax.ppermute(x, axis, plus)
        return [chunks[0], chunks[1]]
    cur_p, cur_m = x, x
    for k in range(1, (n - 1) // 2 + 1):
        cur_p = lax.ppermute(cur_p, axis, plus)
        cur_m = lax.ppermute(cur_m, axis, minus)
        chunks[(-k) % n] = cur_p
        chunks[k] = cur_m
    if n % 2 == 0:
        h = cur_p.shape[0] // 2
        first = lax.ppermute(cur_p[:h], axis, plus)
        second = lax.ppermute(cur_m[h:], axis, minus)
        chunks[n // 2] = jnp.concatenate([first, second], axis=0)
    return [chunks[d] for d in range(n)]


def ladder_kernel(n_chunks, chunk_tiles, tiles_col, bpw, hsel_ref, tab_ref, pos_ref, w_ref, *refs):
    a_refs = refs[:n_chunks]
    m1_ref, m2_ref, o_ref = refs[n_chunks:n_chunks + 3]
    j = pl.program_id(0)
    tn = o_ref.shape[1]
    per = tn // TS
    hr = m1_ref.shape[0] // tab_ref.shape[0]
    first_tile = (hsel_ref[0] * bpw + j) * per
    col_tile = lax.broadcasted_iota(jnp.int32, (1, tn), 1) // TS
    groups_per_chunk = chunk_tiles // GROUP
    for g in range(n_chunks * groups_per_chunk):
        d = g // groups_per_chunk
        off = (g % groups_per_chunk) * GROUP * TS
        pieces = []
        for u in range(GROUP):
            s = tab_ref[g * GROUP + u]
            ps = pos_ref[s]
            top = m1_ref[pl.ds(pl.multiple_of(s * hr, hr), hr), :]
            bottom = m2_ref[pl.ds(pl.multiple_of(ps * hr, hr), hr), :]
            piece = jnp.concatenate([top, bottom], axis=0)
            wv = jnp.zeros((1, tn), jnp.int32)
            for t in range(per):
                wv = jnp.where(col_tile == t, w_ref[s * tiles_col + first_tile + t], wv)
            pieces.append(jnp.where(wv != 0, piece, jnp.zeros_like(piece)))
        mg = jnp.concatenate(pieces, axis=0)
        term = jnp.dot(a_refs[d][:, off:off + GROUP * TS], mg, preferred_element_type=jnp.float32)
        if g == 0:
            o_ref[...] = term
        else:
            o_ref[...] += term


def ladder_matmul(hsel, tab, pos, wflat, amp_chunks, m1, m2, tiles_col, width):
    mrow, ck = amp_chunks[0].shape
    n_chunks = len(amp_chunks)
    kk, ncol = m1.shape
    tn = min(TN, width)
    bpw = width // tn
    kernel = functools.partial(ladder_kernel, n_chunks, ck // TS, tiles_col, bpw)
    a_spec = pl.BlockSpec((mrow, ck), lambda j, h, t, p, w: (0, 0))
    m_spec = pl.BlockSpec((kk, tn), lambda j, h, t, p, w: (0, h[0] * bpw + j))
    return pl.pallas_call(
        kernel,
        out_shape=jax.ShapeDtypeStruct((mrow, width), jnp.float32),
        grid_spec=pltpu.PrefetchScalarGridSpec(
            num_scalar_prefetch=4,
            grid=(bpw,),
            in_specs=[a_spec] * n_chunks + [m_spec, m_spec],
            out_specs=pl.BlockSpec((mrow, tn), lambda j, h, t, p, w: (0, j)),
        ),
        compiler_params=pltpu.CompilerParams(
            dimension_semantics=("arbitrary",), vmem_limit_bytes=56 * 1024 * 1024
        ),
    )(hsel, tab, pos, wflat, *amp_chunks, m1, m2)


def on_device(amplitudes, integrals, tile_mask, k_irrep, n_irrep, stored_tile):
    slab = lax.axis_index("rep")
    column = lax.axis_index("col")
    n_col = lax.axis_size("col")
    nz = lax.axis_size("z")
    nx = lax.axis_size("x")
    n_row = nz * nx
    zi = lax.axis_index("z")
    xi = lax.axis_index("x")

    ncol = integrals.shape[1]
    tiles_col = ncol // TS
    stored_rows = integrals.shape[0]
    slab_tiles = stored_rows * n_row // TS
    mrow = amplitudes.shape[0]
    chunk_tiles = amplitudes.shape[1] // TS

    n_labels = lax.dynamic_slice_in_dim(n_irrep, column * tiles_col, tiles_col)
    mask_cols = lax.dynamic_slice_in_dim(tile_mask, column * tiles_col, tiles_col, 1)
    slots = lax.dynamic_slice_in_dim(stored_tile, slab * slab_tiles, slab_tiles)
    same = jnp.take(k_irrep, slots)[:, None] == n_labels[None, :]
    occupied = jnp.take(mask_cols, slots, axis=0) == 1
    weights = jnp.logical_and(same, occupied).astype(jnp.int32)
    local_ids = slots - slab * slab_tiles
    inverse = jnp.zeros((slab_tiles,), jnp.int32).at[local_ids].set(
        jnp.arange(slab_tiles, dtype=jnp.int32)
    )
    q = jnp.arange(n_col * chunk_tiles, dtype=jnp.int32)
    tab = jnp.take(inverse, ((column + q // chunk_tiles) % n_col) * chunk_tiles + q % chunk_tiles)

    amp_chunks = ring_gather(amplitudes, "col", n_col, n_col, 1)

    assert stored_rows == TS
    hr = stored_rows // 2
    m1 = lax.all_gather(integrals[:hr], ("z", "x"), axis=0, tiled=True)
    xs = ring_gather(integrals[hr:], ("z", "x"), n_row, nx, 1)
    zs = ring_gather(jnp.stack(xs), ("z", "x"), n_row, nz, nx)
    m2 = jnp.stack(zs).reshape(n_row * hr, ncol)
    sl = jnp.arange(slab_tiles, dtype=jnp.int32)
    pos = ((sl // nx - zi) % nz) * nx + (sl % nx - xi) % nx

    n_rep = lax.axis_size("rep")
    width = ncol // n_rep
    wflat = weights.reshape(-1)
    other = (1 - slab).astype(jnp.int32).reshape(1)
    own = slab.astype(jnp.int32).reshape(1)
    send = ladder_matmul(other, tab, pos, wflat, amp_chunks, m1, m2, tiles_col, width)
    got = lax.ppermute(send, "rep", [(0, 1), (1, 0)])
    keep = ladder_matmul(own, tab, pos, wflat, amp_chunks, m1, m2, tiles_col, width)
    return (keep + got).astype(jnp.bfloat16)


def solution(mesh):
    nrow = mesh.shape["row"]
    nx = X_RING if nrow % X_RING == 0 else 1
    devices = mesh.devices.reshape(nrow // nx, nx, mesh.shape["col"], mesh.shape["rep"])
    fine = Mesh(devices, ("z", "x", "col", "rep"))
    rows = ("z", "x")
    placed = (P(rows, ("rep", "col")), P(("rep",) + rows, "col"), P(), P(), P(), P())
    return jax.shard_map(
        on_device, mesh=fine, in_specs=placed, out_specs=P(rows, ("col", "rep")), check_vma=False
    )
```

```python
import functools

import jax
import jax.numpy as jnp
from jax import lax
from jax.experimental import pallas as pl
from jax.experimental.pallas import tpu as pltpu
from jax.sharding import Mesh, PartitionSpec as P

TS = 128
X_RING = 4
GROUP = 4
TN = 256


def ring_perm(total, n, stride, step):
    pairs = []
    for i in range(total):
        base = (i // (stride * n)) * (stride * n) + i % stride
        pos = (i // stride) % n
        pairs.append((i, base + ((pos + step) % n) * stride))
    return pairs


def ring_gather(x, axis, total, n, stride):
    if n == 1:
        return [x]
    plus = ring_perm(total, n, stride, 1)
    minus = ring_perm(total, n, stride, -1)
    chunks = {0: x}
    if n == 2:
        chunks[1] = lax.ppermute(x, axis, plus)
        return [chunks[0], chunks[1]]
    cur_p, cur_m = x, x
    for k in range(1, (n - 1) // 2 + 1):
        cur_p = lax.ppermute(cur_p, axis, plus)
        cur_m = lax.ppermute(cur_m, axis, minus)
        chunks[(-k) % n] = cur_p
        chunks[k] = cur_m
    if n % 2 == 0:
        h = cur_p.shape[0] // 2
        first = lax.ppermute(cur_p[:h], axis, plus)
        second = lax.ppermute(cur_m[h:], axis, minus)
        chunks[n // 2] = jnp.concatenate([first, second], axis=0)
    return [chunks[d] for d in range(n)]


def ladder_kernel(chunk_tiles, tiles_col, hsel_ref, tab_ref, pos_ref, w_ref, *refs):
    n_chunks = len(refs) - 5
    a_hbm = refs[:n_chunks]
    m1_ref, m2_ref, o_ref, abuf, sem = refs[n_chunks:]
    tn = o_ref.shape[1]
    per = tn // TS
    hr = m1_ref.shape[0] // tab_ref.shape[0]
    first_tile = hsel_ref[0] * per
    col_tile = lax.broadcasted_iota(jnp.int32, (1, tn), 1) // TS

    def copy(k):
        return pltpu.make_async_copy(a_hbm[k], abuf.at[k % 2], sem.at[k % 2])

    copy(0).start()
    for k in range(n_chunks):
        if k + 1 < n_chunks:
            copy(k + 1).start()
        pieces = []
        for u in range(chunk_tiles):
            s = tab_ref[k * chunk_tiles + u]
            ps = pos_ref[s]
            top = m1_ref[pl.ds(pl.multiple_of(s * hr, hr), hr), :]
            bottom = m2_ref[pl.ds(pl.multiple_of(ps * hr, hr), hr), :]
            piece = jnp.concatenate([top, bottom], axis=0)
            wv = jnp.zeros((1, tn), jnp.int32)
            for t in range(per):
                wv = jnp.where(col_tile == t, w_ref[s * tiles_col + first_tile + t], wv)
            pieces.append(jnp.where(wv != 0, piece, jnp.zeros_like(piece)))
        mg = jnp.concatenate(pieces, axis=0)
        copy(k).wait()
        term = jnp.dot(abuf[k % 2], mg, preferred_element_type=jnp.float32)
        if k == 0:
            o_ref[...] = term
        else:
            o_ref[...] += term


def ladder_matmul(hsel, tab, pos, wflat, amp_chunks, m1, m2, tiles_col, width):
    mrow, ck = amp_chunks[0].shape
    n_chunks = len(amp_chunks)
    kk, ncol = m1.shape
    kernel = functools.partial(ladder_kernel, ck // TS, tiles_col)
    m_spec = pl.BlockSpec((kk, width), lambda i, h, t, p, w: (0, h[0]))
    return pl.pallas_call(
        kernel,
        out_shape=jax.ShapeDtypeStruct((mrow, width), jnp.float32),
        grid_spec=pltpu.PrefetchScalarGridSpec(
            num_scalar_prefetch=4,
            grid=(1,),
            in_specs=[pl.BlockSpec(memory_space=pl.ANY)] * n_chunks + [m_spec, m_spec],
            out_specs=pl.BlockSpec((mrow, width), lambda i, h, t, p, w: (0, 0)),
            scratch_shapes=[pltpu.VMEM((2, mrow, ck), amp_chunks[0].dtype), pltpu.SemaphoreType.DMA((2,))],
        ),
        compiler_params=pltpu.CompilerParams(
            dimension_semantics=("arbitrary",), vmem_limit_bytes=56 * 1024 * 1024
        ),
    )(hsel, tab, pos, wflat, *amp_chunks, m1, m2)


def on_device(amplitudes, integrals, tile_mask, k_irrep, n_irrep, stored_tile):
    slab = lax.axis_index("rep")
    column = lax.axis_index("col")
    n_col = lax.axis_size("col")
    nz = lax.axis_size("z")
    nx = lax.axis_size("x")
    n_row = nz * nx
    zi = lax.axis_index("z")
    xi = lax.axis_index("x")

    ncol = integrals.shape[1]
    tiles_col = ncol // TS
    stored_rows = integrals.shape[0]
    slab_tiles = stored_rows * n_row // TS
    mrow = amplitudes.shape[0]
    chunk_tiles = amplitudes.shape[1] // TS

    n_labels = lax.dynamic_slice_in_dim(n_irrep, column * tiles_col, tiles_col)
    mask_cols = lax.dynamic_slice_in_dim(tile_mask, column * tiles_col, tiles_col, 1)
    slots = lax.dynamic_slice_in_dim(stored_tile, slab * slab_tiles, slab_tiles)
    same = jnp.take(k_irrep, slots)[:, None] == n_labels[None, :]
    occupied = jnp.take(mask_cols, slots, axis=0) == 1
    weights = jnp.logical_and(same, occupied).astype(jnp.int32)
    local_ids = slots - slab * slab_tiles
    inverse = jnp.zeros((slab_tiles,), jnp.int32).at[local_ids].set(
        jnp.arange(slab_tiles, dtype=jnp.int32)
    )
    q = jnp.arange(n_col * chunk_tiles, dtype=jnp.int32)
    tab = jnp.take(inverse, ((column + q // chunk_tiles) % n_col) * chunk_tiles + q % chunk_tiles)

    amp_chunks = ring_gather(amplitudes, "col", n_col, n_col, 1)

    assert stored_rows == TS
    hr = stored_rows // 2
    m1 = lax.all_gather(integrals[:hr], ("z", "x"), axis=0, tiled=True)
    xs = ring_gather(integrals[hr:], ("z", "x"), n_row, nx, 1)
    zs = ring_gather(jnp.stack(xs), ("z", "x"), n_row, nz, nx)
    m2 = jnp.stack(zs).reshape(n_row * hr, ncol)
    sl = jnp.arange(slab_tiles, dtype=jnp.int32)
    pos = ((sl // nx - zi) % nz) * nx + (sl % nx - xi) % nx

    n_rep = lax.axis_size("rep")
    width = ncol // n_rep
    wflat = weights.reshape(-1)
    other = (1 - slab).astype(jnp.int32).reshape(1)
    own = slab.astype(jnp.int32).reshape(1)
    send = ladder_matmul(other, tab, pos, wflat, amp_chunks, m1, m2, tiles_col, width)
    got = lax.ppermute(send, "rep", [(0, 1), (1, 0)])
    keep = ladder_matmul(own, tab, pos, wflat, amp_chunks, m1, m2, tiles_col, width)
    return (keep + got).astype(jnp.bfloat16)


def solution(mesh):
    nrow = mesh.shape["row"]
    nx = X_RING if nrow % X_RING == 0 else 1
    devices = mesh.devices.reshape(nrow // nx, nx, mesh.shape["col"], mesh.shape["rep"])
    fine = Mesh(devices, ("z", "x", "col", "rep"))
    rows = ("z", "x")
    placed = (P(rows, ("rep", "col")), P(("rep",) + rows, "col"), P(), P(), P(), P())
    return jax.shard_map(
        on_device, mesh=fine, in_specs=placed, out_specs=P(rows, ("col", "rep")), check_vma=False
    )
```

```python
import functools

import jax
import jax.numpy as jnp
from jax import lax
from jax.experimental import pallas as pl
from jax.experimental.pallas import tpu as pltpu
from jax.sharding import Mesh, PartitionSpec as P

TS = 128
X_RING = 4
GROUP = 4
TN = 256
RB = 256


def ring_perm(total, n, stride, step):
    pairs = []
    for i in range(total):
        base = (i // (stride * n)) * (stride * n) + i % stride
        pos = (i // stride) % n
        pairs.append((i, base + ((pos + step) % n) * stride))
    return pairs


def ring_gather(x, axis, total, n, stride):
    if n == 1:
        return [x]
    plus = ring_perm(total, n, stride, 1)
    minus = ring_perm(total, n, stride, -1)
    chunks = {0: x}
    if n == 2:
        chunks[1] = lax.ppermute(x, axis, plus)
        return [chunks[0], chunks[1]]
    cur_p, cur_m = x, x
    for k in range(1, (n - 1) // 2 + 1):
        cur_p = lax.ppermute(cur_p, axis, plus)
        cur_m = lax.ppermute(cur_m, axis, minus)
        chunks[(-k) % n] = cur_p
        chunks[k] = cur_m
    if n % 2 == 0:
        h = cur_p.shape[0] // 2
        first = lax.ppermute(cur_p[:h], axis, plus)
        second = lax.ppermute(cur_m[h:], axis, minus)
        chunks[n // 2] = jnp.concatenate([first, second], axis=0)
    return [chunks[d] for d in range(n)]


def ladder_kernel(chunk_tiles, tiles_col, hsel_ref, tab_ref, pos_ref, w_ref, *refs):
    n_chunks = len(refs) - 6
    a_hbm = refs[:n_chunks]
    m1_ref, m2_ref, o_ref, abuf, sem, mg_ref = refs[n_chunks:]
    tn = o_ref.shape[1]
    per = tn // TS
    hr = m1_ref.shape[0] // tab_ref.shape[0]
    first_tile = hsel_ref[0] * per
    col_tile = lax.broadcasted_iota(jnp.int32, (1, tn), 1) // TS

    def copy(k):
        return pltpu.make_async_copy(a_hbm[k], abuf.at[k % 2], sem.at[k % 2])

    copy(0).start()
    mrow = o_ref.shape[0]
    rb = min(RB, mrow)
    for k in range(n_chunks):
        if k + 1 < n_chunks:
            copy(k + 1).start()
        for u in range(chunk_tiles):
            s = tab_ref[k * chunk_tiles + u]
            ps = pos_ref[s]
            top = m1_ref[pl.ds(pl.multiple_of(s * hr, hr), hr), :]
            bottom = m2_ref[pl.ds(pl.multiple_of(ps * hr, hr), hr), :]
            wv = jnp.zeros((1, tn), jnp.int32)
            for t in range(per):
                wv = jnp.where(col_tile == t, w_ref[s * tiles_col + first_tile + t], wv)
            keep = wv != 0
            mg_ref[u * TS:u * TS + hr, :] = jnp.where(keep, top, jnp.zeros_like(top))
            mg_ref[u * TS + hr:(u + 1) * TS, :] = jnp.where(keep, bottom, jnp.zeros_like(bottom))
        copy(k).wait()
        for r in range(mrow // rb):
            term = jnp.dot(abuf[k % 2, r * rb:(r + 1) * rb, :], mg_ref[...], preferred_element_type=jnp.float32)
            if k == 0:
                o_ref[r * rb:(r + 1) * rb, :] = term
            else:
                o_ref[r * rb:(r + 1) * rb, :] += term


def ladder_matmul(hsel, tab, pos, wflat, amp_chunks, m1, m2, tiles_col, width):
    mrow, ck = amp_chunks[0].shape
    n_chunks = len(amp_chunks)
    kk, ncol = m1.shape
    kernel = functools.partial(ladder_kernel, ck // TS, tiles_col)
    m_spec = pl.BlockSpec((kk, width), lambda i, h, t, p, w: (0, h[0]))
    return pl.pallas_call(
        kernel,
        out_shape=jax.ShapeDtypeStruct((mrow, width), jnp.float32),
        grid_spec=pltpu.PrefetchScalarGridSpec(
            num_scalar_prefetch=4,
            grid=(1,),
            in_specs=[pl.BlockSpec(memory_space=pl.ANY)] * n_chunks + [m_spec, m_spec],
            out_specs=pl.BlockSpec((mrow, width), lambda i, h, t, p, w: (0, 0)),
            scratch_shapes=[pltpu.VMEM((2, mrow, ck), amp_chunks[0].dtype), pltpu.SemaphoreType.DMA((2,)),
                            pltpu.VMEM((ck, width), m1.dtype)],
        ),
        compiler_params=pltpu.CompilerParams(
            dimension_semantics=("arbitrary",), vmem_limit_bytes=56 * 1024 * 1024
        ),
    )(hsel, tab, pos, wflat, *amp_chunks, m1, m2)


def on_device(amplitudes, integrals, tile_mask, k_irrep, n_irrep, stored_tile):
    slab = lax.axis_index("rep")
    column = lax.axis_index("col")
    n_col = lax.axis_size("col")
    nz = lax.axis_size("z")
    nx = lax.axis_size("x")
    n_row = nz * nx
    zi = lax.axis_index("z")
    xi = lax.axis_index("x")

    ncol = integrals.shape[1]
    tiles_col = ncol // TS
    stored_rows = integrals.shape[0]
    slab_tiles = stored_rows * n_row // TS
    mrow = amplitudes.shape[0]
    chunk_tiles = amplitudes.shape[1] // TS

    n_labels = lax.dynamic_slice_in_dim(n_irrep, column * tiles_col, tiles_col)
    mask_cols = lax.dynamic_slice_in_dim(tile_mask, column * tiles_col, tiles_col, 1)
    slots = lax.dynamic_slice_in_dim(stored_tile, slab * slab_tiles, slab_tiles)
    same = jnp.take(k_irrep, slots)[:, None] == n_labels[None, :]
    occupied = jnp.take(mask_cols, slots, axis=0) == 1
    weights = jnp.logical_and(same, occupied).astype(jnp.int32)
    local_ids = slots - slab * slab_tiles
    inverse = jnp.zeros((slab_tiles,), jnp.int32).at[local_ids].set(
        jnp.arange(slab_tiles, dtype=jnp.int32)
    )
    q = jnp.arange(n_col * chunk_tiles, dtype=jnp.int32)
    tab = jnp.take(inverse, ((column + q // chunk_tiles) % n_col) * chunk_tiles + q % chunk_tiles)

    amp_chunks = ring_gather(amplitudes, "col", n_col, n_col, 1)

    assert stored_rows == TS
    hr = stored_rows // 2
    m1 = lax.all_gather(integrals[:hr], ("z", "x"), axis=0, tiled=True)
    xs = ring_gather(integrals[hr:], ("z", "x"), n_row, nx, 1)
    zs = ring_gather(jnp.stack(xs), ("z", "x"), n_row, nz, nx)
    m2 = jnp.stack(zs).reshape(n_row * hr, ncol)
    sl = jnp.arange(slab_tiles, dtype=jnp.int32)
    pos = ((sl // nx - zi) % nz) * nx + (sl % nx - xi) % nx

    n_rep = lax.axis_size("rep")
    width = ncol // n_rep
    wflat = weights.reshape(-1)
    other = (1 - slab).astype(jnp.int32).reshape(1)
    own = slab.astype(jnp.int32).reshape(1)
    send = ladder_matmul(other, tab, pos, wflat, amp_chunks, m1, m2, tiles_col, width)
    got = lax.ppermute(send, "rep", [(0, 1), (1, 0)])
    keep = ladder_matmul(own, tab, pos, wflat, amp_chunks, m1, m2, tiles_col, width)
    return (keep + got).astype(jnp.bfloat16)


def solution(mesh):
    nrow = mesh.shape["row"]
    nx = X_RING if nrow % X_RING == 0 else 1
    devices = mesh.devices.reshape(nrow // nx, nx, mesh.shape["col"], mesh.shape["rep"])
    fine = Mesh(devices, ("z", "x", "col", "rep"))
    rows = ("z", "x")
    placed = (P(rows, ("rep", "col")), P(("rep",) + rows, "col"), P(), P(), P(), P())
    return jax.shard_map(
        on_device, mesh=fine, in_specs=placed, out_specs=P(rows, ("col", "rep")), check_vma=False
    )
```

```python
import functools

import jax
import jax.numpy as jnp
from jax import lax
from jax.experimental import pallas as pl
from jax.experimental.pallas import tpu as pltpu
from jax.sharding import Mesh, PartitionSpec as P

TS = 128
X_RING = 4
GROUP = 4
TN = 256
TM = 256


def ring_perm(total, n, stride, step):
    pairs = []
    for i in range(total):
        base = (i // (stride * n)) * (stride * n) + i % stride
        pos = (i // stride) % n
        pairs.append((i, base + ((pos + step) % n) * stride))
    return pairs


def ring_gather(x, axis, total, n, stride):
    if n == 1:
        return [x]
    plus = ring_perm(total, n, stride, 1)
    minus = ring_perm(total, n, stride, -1)
    chunks = {0: x}
    if n == 2:
        chunks[1] = lax.ppermute(x, axis, plus)
        return [chunks[0], chunks[1]]
    cur_p, cur_m = x, x
    for k in range(1, (n - 1) // 2 + 1):
        cur_p = lax.ppermute(cur_p, axis, plus)
        cur_m = lax.ppermute(cur_m, axis, minus)
        chunks[(-k) % n] = cur_p
        chunks[k] = cur_m
    if n % 2 == 0:
        h = cur_p.shape[0] // 2
        first = lax.ppermute(cur_p[:h], axis, plus)
        second = lax.ppermute(cur_m[h:], axis, minus)
        chunks[n // 2] = jnp.concatenate([first, second], axis=0)
    return [chunks[d] for d in range(n)]


def ladder_kernel(chunk_tiles, tiles_col, hsel_ref, tab_ref, pos_ref, w_ref, *refs):
    n_chunks = len(refs) - 4
    a_refs = refs[:n_chunks]
    m1_ref, m2_ref, o_ref, mg_ref = refs[n_chunks:]
    tn = o_ref.shape[1]
    per = tn // TS
    hr = m1_ref.shape[0] // tab_ref.shape[0]
    first_tile = hsel_ref[0] * per
    ck = chunk_tiles * TS

    @pl.when(pl.program_id(0) == 0)
    def _():
        col_tile = lax.broadcasted_iota(jnp.int32, (1, tn), 1) // TS
        for q in range(n_chunks * chunk_tiles):
            s = tab_ref[q]
            ps = pos_ref[s]
            top = m1_ref[pl.ds(pl.multiple_of(s * hr, hr), hr), :]
            bottom = m2_ref[pl.ds(pl.multiple_of(ps * hr, hr), hr), :]
            wv = jnp.zeros((1, tn), jnp.int32)
            for t in range(per):
                wv = jnp.where(col_tile == t, w_ref[s * tiles_col + first_tile + t], wv)
            keep = wv != 0
            mg_ref[q * TS:q * TS + hr, :] = jnp.where(keep, top, jnp.zeros_like(top))
            mg_ref[q * TS + hr:(q + 1) * TS, :] = jnp.where(keep, bottom, jnp.zeros_like(bottom))

    acc = None
    for k in range(n_chunks):
        term = jnp.dot(a_refs[k][...], mg_ref[k * ck:(k + 1) * ck, :], preferred_element_type=jnp.float32)
        acc = term if acc is None else acc + term
    o_ref[...] = acc


def ladder_matmul(hsel, tab, pos, wflat, amp_chunks, m1, m2, tiles_col, width):
    mrow, ck = amp_chunks[0].shape
    n_chunks = len(amp_chunks)
    kk, ncol = m1.shape
    tm = min(TM, mrow)
    kernel = functools.partial(ladder_kernel, ck // TS, tiles_col)
    m_spec = pl.BlockSpec((kk, width), lambda i, h, t, p, w: (0, h[0]))
    a_spec = pl.BlockSpec((tm, ck), lambda i, h, t, p, w: (i, 0))
    return pl.pallas_call(
        kernel,
        out_shape=jax.ShapeDtypeStruct((mrow, width), jnp.float32),
        grid_spec=pltpu.PrefetchScalarGridSpec(
            num_scalar_prefetch=4,
            grid=(mrow // tm,),
            in_specs=[a_spec] * n_chunks + [m_spec, m_spec],
            out_specs=pl.BlockSpec((tm, width), lambda i, h, t, p, w: (i, 0)),
            scratch_shapes=[pltpu.VMEM((n_chunks * ck, width), m1.dtype)],
        ),
        compiler_params=pltpu.CompilerParams(
            dimension_semantics=("arbitrary",), vmem_limit_bytes=56 * 1024 * 1024
        ),
    )(hsel, tab, pos, wflat, *amp_chunks, m1, m2)


def on_device(amplitudes, integrals, tile_mask, k_irrep, n_irrep, stored_tile):
    slab = lax.axis_index("rep")
    column = lax.axis_index("col")
    n_col = lax.axis_size("col")
    nz = lax.axis_size("z")
    nx = lax.axis_size("x")
    n_row = nz * nx
    zi = lax.axis_index("z")
    xi = lax.axis_index("x")

    ncol = integrals.shape[1]
    tiles_col = ncol // TS
    stored_rows = integrals.shape[0]
    slab_tiles = stored_rows * n_row // TS
    mrow = amplitudes.shape[0]
    chunk_tiles = amplitudes.shape[1] // TS

    n_labels = lax.dynamic_slice_in_dim(n_irrep, column * tiles_col, tiles_col)
    mask_cols = lax.dynamic_slice_in_dim(tile_mask, column * tiles_col, tiles_col, 1)
    slots = lax.dynamic_slice_in_dim(stored_tile, slab * slab_tiles, slab_tiles)
    same = jnp.take(k_irrep, slots)[:, None] == n_labels[None, :]
    occupied = jnp.take(mask_cols, slots, axis=0) == 1
    weights = jnp.logical_and(same, occupied).astype(jnp.int32)
    local_ids = slots - slab * slab_tiles
    inverse = jnp.zeros((slab_tiles,), jnp.int32).at[local_ids].set(
        jnp.arange(slab_tiles, dtype=jnp.int32)
    )
    q = jnp.arange(n_col * chunk_tiles, dtype=jnp.int32)
    tab = jnp.take(inverse, ((column + q // chunk_tiles) % n_col) * chunk_tiles + q % chunk_tiles)

    amp_chunks = ring_gather(amplitudes, "col", n_col, n_col, 1)

    assert stored_rows == TS
    hr = stored_rows // 2
    m1 = lax.all_gather(integrals[:hr], ("z", "x"), axis=0, tiled=True)
    xs = ring_gather(integrals[hr:], ("z", "x"), n_row, nx, 1)
    zs = ring_gather(jnp.stack(xs), ("z", "x"), n_row, nz, nx)
    m2 = jnp.stack(zs).reshape(n_row * hr, ncol)
    sl = jnp.arange(slab_tiles, dtype=jnp.int32)
    pos = ((sl // nx - zi) % nz) * nx + (sl % nx - xi) % nx

    n_rep = lax.axis_size("rep")
    width = ncol // n_rep
    wflat = weights.reshape(-1)
    other = (1 - slab).astype(jnp.int32).reshape(1)
    own = slab.astype(jnp.int32).reshape(1)
    send = ladder_matmul(other, tab, pos, wflat, amp_chunks, m1, m2, tiles_col, width)
    got = lax.ppermute(send, "rep", [(0, 1), (1, 0)])
    keep = ladder_matmul(own, tab, pos, wflat, amp_chunks, m1, m2, tiles_col, width)
    return (keep + got).astype(jnp.bfloat16)


def solution(mesh):
    nrow = mesh.shape["row"]
    nx = X_RING if nrow % X_RING == 0 else 1
    devices = mesh.devices.reshape(nrow // nx, nx, mesh.shape["col"], mesh.shape["rep"])
    fine = Mesh(devices, ("z", "x", "col", "rep"))
    rows = ("z", "x")
    placed = (P(rows, ("rep", "col")), P(("rep",) + rows, "col"), P(), P(), P(), P())
    return jax.shard_map(
        on_device, mesh=fine, in_specs=placed, out_specs=P(rows, ("col", "rep")), check_vma=False
    )
```

```python
import functools

import jax
import jax.numpy as jnp
from jax import lax
from jax.experimental import pallas as pl
from jax.experimental.pallas import tpu as pltpu
from jax.sharding import Mesh, PartitionSpec as P

TS = 128
X_RING = 4
GROUP = 4
TN = 256
TM = 256


def ring_perm(total, n, stride, step):
    pairs = []
    for i in range(total):
        base = (i // (stride * n)) * (stride * n) + i % stride
        pos = (i // stride) % n
        pairs.append((i, base + ((pos + step) % n) * stride))
    return pairs


class Ring:
    def __init__(self, x, axis, total, n, stride):
        self.axis, self.n = axis, n
        self.plus = ring_perm(total, n, stride, 1)
        self.minus = ring_perm(total, n, stride, -1)
        self.chunks = {0: x}
        self.cur_p, self.cur_m = x, x
        self.k = 0
        self.steps = 0 if n == 1 else (n - 1) // 2 + (1 if n % 2 == 0 else 0)

    def step(self):
        self.k += 1
        k, n = self.k, self.n
        if n == 2:
            self.chunks[1] = lax.ppermute(self.cur_p, self.axis, self.plus)
        elif k <= (n - 1) // 2:
            self.cur_p = lax.ppermute(self.cur_p, self.axis, self.plus)
            self.cur_m = lax.ppermute(self.cur_m, self.axis, self.minus)
            self.chunks[(-k) % n] = self.cur_p
            self.chunks[k] = self.cur_m
        else:
            h = self.cur_p.shape[0] // 2
            first = lax.ppermute(self.cur_p[:h], self.axis, self.plus)
            second = lax.ppermute(self.cur_m[h:], self.axis, self.minus)
            self.chunks[n // 2] = jnp.concatenate([first, second], axis=0)

    def result(self):
        return jnp.stack([self.chunks[d] for d in range(self.n)])


def ladder_kernel(chunk_tiles, tiles_col, hsel_ref, tab_ref, pos_ref, w_ref, *refs):
    n_chunks = len(refs) - 3
    a_refs = refs[:n_chunks]
    m_ref, o_ref, mg_ref = refs[n_chunks:]
    tn = o_ref.shape[1]
    per = tn // TS
    first_tile = hsel_ref[0] * per
    ck = chunk_tiles * TS

    @pl.when(pl.program_id(0) == 0)
    def _():
        col_tile = lax.broadcasted_iota(jnp.int32, (1, tn), 1) // TS
        for q in range(n_chunks * chunk_tiles):
            s = tab_ref[q]
            piece = m_ref[pl.ds(pl.multiple_of(pos_ref[s] * TS, TS), TS), :]
            wv = jnp.zeros((1, tn), jnp.int32)
            for t in range(per):
                wv = jnp.where(col_tile == t, w_ref[s * tiles_col + first_tile + t], wv)
            mg_ref[q * TS:(q + 1) * TS, :] = jnp.where(wv != 0, piece, jnp.zeros_like(piece))

    acc = None
    for k in range(n_chunks):
        term = jnp.dot(a_refs[k][...], mg_ref[k * ck:(k + 1) * ck, :], preferred_element_type=jnp.float32)
        acc = term if acc is None else acc + term
    o_ref[...] = acc


def ladder_matmul(hsel, tab, pos, wflat, amp_chunks, m_all, tiles_col):
    mrow, ck = amp_chunks[0].shape
    n_chunks = len(amp_chunks)
    kk, width = m_all.shape
    tm = min(TM, mrow)
    kernel = functools.partial(ladder_kernel, ck // TS, tiles_col)
    a_spec = pl.BlockSpec((tm, ck), lambda i, h, t, p, w: (i, 0))
    return pl.pallas_call(
        kernel,
        out_shape=jax.ShapeDtypeStruct((mrow, width), jnp.float32),
        grid_spec=pltpu.PrefetchScalarGridSpec(
            num_scalar_prefetch=4,
            grid=(mrow // tm,),
            in_specs=[a_spec] * n_chunks + [pl.BlockSpec((kk, width), lambda i, h, t, p, w: (0, 0))],
            out_specs=pl.BlockSpec((tm, width), lambda i, h, t, p, w: (i, 0)),
            scratch_shapes=[pltpu.VMEM((n_chunks * ck, width), m_all.dtype)],
        ),
        compiler_params=pltpu.CompilerParams(
            dimension_semantics=("arbitrary",), vmem_limit_bytes=56 * 1024 * 1024
        ),
    )(hsel, tab, pos, wflat, *amp_chunks, m_all)


def on_device(amplitudes, integrals, tile_mask, k_irrep, n_irrep, stored_tile):
    slab = lax.axis_index("rep")
    column = lax.axis_index("col")
    n_col = lax.axis_size("col")
    nz = lax.axis_size("z")
    nx = lax.axis_size("x")
    n_row = nz * nx
    zi = lax.axis_index("z")
    xi = lax.axis_index("x")

    ncol = integrals.shape[1]
    tiles_col = ncol // TS
    stored_rows = integrals.shape[0]
    slab_tiles = stored_rows * n_row // TS
    mrow = amplitudes.shape[0]
    chunk_tiles = amplitudes.shape[1] // TS

    n_labels = lax.dynamic_slice_in_dim(n_irrep, column * tiles_col, tiles_col)
    mask_cols = lax.dynamic_slice_in_dim(tile_mask, column * tiles_col, tiles_col, 1)
    slots = lax.dynamic_slice_in_dim(stored_tile, slab * slab_tiles, slab_tiles)
    same = jnp.take(k_irrep, slots)[:, None] == n_labels[None, :]
    occupied = jnp.take(mask_cols, slots, axis=0) == 1
    weights = jnp.logical_and(same, occupied).astype(jnp.int32)
    local_ids = slots - slab * slab_tiles
    inverse = jnp.zeros((slab_tiles,), jnp.int32).at[local_ids].set(
        jnp.arange(slab_tiles, dtype=jnp.int32)
    )
    q = jnp.arange(n_col * chunk_tiles, dtype=jnp.int32)
    tab = jnp.take(inverse, ((column + q // chunk_tiles) % n_col) * chunk_tiles + q % chunk_tiles)

    n_rep = lax.axis_size("rep")
    width = ncol // n_rep
    wflat = weights.reshape(-1)
    other = (1 - slab).astype(jnp.int32).reshape(1)
    own = slab.astype(jnp.int32).reshape(1)
    rows = ("z", "x")

    plus = ring_perm(n_col, n_col, 1, 1)
    minus = ring_perm(n_col, n_col, 1, -1)
    from_left = lax.ppermute(amplitudes, "col", plus)
    from_right = lax.ppermute(amplitudes, "col", minus)

    send_cols = lax.dynamic_slice_in_dim(integrals, other[0] * width, width, 1)
    own_cols = lax.dynamic_slice_in_dim(integrals, own[0] * width, width, 1)
    m_own = lax.all_gather(own_cols, rows, axis=0, tiled=True)
    short = Ring(send_cols, rows, n_row, nx, 1)
    for _ in range(short.steps):
        short.step()
    ring = Ring(short.result(), rows, n_row, nz, nx)
    far = None
    for i in range(ring.steps):
        ring.step()
        if i + 1 == 2:
            ring.cur_p, ring.cur_m, from_left, from_right = lax.optimization_barrier(
                (ring.cur_p, ring.cur_m, from_left, from_right)
            )
            ha = mrow // 2
            far = jnp.concatenate(
                [lax.ppermute(from_left[:ha], "col", plus), lax.ppermute(from_right[ha:], "col", minus)],
                axis=0,
            )
        if i + 1 == 3:
            ring.cur_p, ring.cur_m, far = lax.optimization_barrier((ring.cur_p, ring.cur_m, far))
    m_send = ring.result().reshape(n_row * stored_rows, width)
    sl = jnp.arange(slab_tiles, dtype=jnp.int32)
    pos_ring = ((sl // nx - zi) % nz) * nx + (sl % nx - xi) % nx
    chunks = [amplitudes, from_right, far, from_left]

    send = ladder_matmul(other, tab, pos_ring, wflat, chunks, m_send, tiles_col)
    got = lax.ppermute(send, "rep", [(0, 1), (1, 0)])
    keep = ladder_matmul(own, tab, sl, wflat, chunks, m_own, tiles_col)
    return (keep + got).astype(jnp.bfloat16)


def solution(mesh):
    nrow = mesh.shape["row"]
    nx = X_RING if nrow % X_RING == 0 else 1
    devices = mesh.devices.reshape(nrow // nx, nx, mesh.shape["col"], mesh.shape["rep"])
    fine = Mesh(devices, ("z", "x", "col", "rep"))
    rows = ("z", "x")
    placed = (P(rows, ("rep", "col")), P(("rep",) + rows, "col"), P(), P(), P(), P())
    return jax.shard_map(
        on_device, mesh=fine, in_specs=placed, out_specs=P(rows, ("col", "rep")), check_vma=False
    )
```

```python
import functools

import jax
import jax.numpy as jnp
from jax import lax
from jax.experimental import pallas as pl
from jax.experimental.pallas import tpu as pltpu
from jax.sharding import Mesh, PartitionSpec as P

TS = 128
X_RING = 4
GROUP = 4
TN = 256
TM = 256


def ring_perm(total, n, stride, step):
    pairs = []
    for i in range(total):
        base = (i // (stride * n)) * (stride * n) + i % stride
        pos = (i // stride) % n
        pairs.append((i, base + ((pos + step) % n) * stride))
    return pairs


def ring_gather(x, axis, total, n, stride):
    if n == 1:
        return [x]
    plus = ring_perm(total, n, stride, 1)
    minus = ring_perm(total, n, stride, -1)
    chunks = {0: x}
    if n == 2:
        chunks[1] = lax.ppermute(x, axis, plus)
        return [chunks[0], chunks[1]]
    cur_p, cur_m = x, x
    for k in range(1, (n - 1) // 2 + 1):
        cur_p = lax.ppermute(cur_p, axis, plus)
        cur_m = lax.ppermute(cur_m, axis, minus)
        chunks[(-k) % n] = cur_p
        chunks[k] = cur_m
    if n % 2 == 0:
        h = cur_p.shape[0] // 2
        first = lax.ppermute(cur_p[:h], axis, plus)
        second = lax.ppermute(cur_m[h:], axis, minus)
        chunks[n // 2] = jnp.concatenate([first, second], axis=0)
    return [chunks[d] for d in range(n)]


def ladder_kernel(chunk_tiles, tiles_col, hsel_ref, tab_ref, pos_ref, w_ref, *refs):
    n_chunks = len(refs) - 4
    a_refs = refs[:n_chunks]
    m1_ref, m2_ref, o_ref, mg_ref = refs[n_chunks:]
    tn = o_ref.shape[1]
    per = tn // TS
    hr = m1_ref.shape[0] // tab_ref.shape[0]
    first_tile = hsel_ref[0] * per
    ck = chunk_tiles * TS

    @pl.when(pl.program_id(0) == 0)
    def _():
        col_tile = lax.broadcasted_iota(jnp.int32, (1, tn), 1) // TS
        for q in range(n_chunks * chunk_tiles):
            s = tab_ref[q]
            p1 = pos_ref[s]
            ps = pos_ref[tab_ref.shape[0] + s]
            top = m1_ref[pl.ds(pl.multiple_of(p1 * hr, hr), hr), :]
            bottom = m2_ref[pl.ds(pl.multiple_of(ps * hr, hr), hr), :]
            wv = jnp.zeros((1, tn), jnp.int32)
            for t in range(per):
                wv = jnp.where(col_tile == t, w_ref[s * tiles_col + first_tile + t], wv)
            keep = wv != 0
            mg_ref[q * TS:q * TS + hr, :] = jnp.where(keep, top, jnp.zeros_like(top))
            mg_ref[q * TS + hr:(q + 1) * TS, :] = jnp.where(keep, bottom, jnp.zeros_like(bottom))

    acc = None
    for k in range(n_chunks):
        term = jnp.dot(a_refs[k][...], mg_ref[k * ck:(k + 1) * ck, :], preferred_element_type=jnp.float32)
        acc = term if acc is None else acc + term
    o_ref[...] = acc


def ladder_matmul(hsel, tab, pos, wflat, amp_chunks, m1, m2, tiles_col, width):
    mrow, ck = amp_chunks[0].shape
    n_chunks = len(amp_chunks)
    kk, ncol = m1.shape
    tm = min(TM, mrow)
    kernel = functools.partial(ladder_kernel, ck // TS, tiles_col)
    m_spec = pl.BlockSpec((kk, width), lambda i, h, t, p, w: (0, h[0]))
    a_spec = pl.BlockSpec((tm, ck), lambda i, h, t, p, w: (i, 0))
    return pl.pallas_call(
        kernel,
        out_shape=jax.ShapeDtypeStruct((mrow, width), jnp.float32),
        grid_spec=pltpu.PrefetchScalarGridSpec(
            num_scalar_prefetch=4,
            grid=(mrow // tm,),
            in_specs=[a_spec] * n_chunks + [m_spec, m_spec],
            out_specs=pl.BlockSpec((tm, width), lambda i, h, t, p, w: (i, 0)),
            scratch_shapes=[pltpu.VMEM((n_chunks * ck, width), m1.dtype)],
        ),
        compiler_params=pltpu.CompilerParams(
            dimension_semantics=("arbitrary",), vmem_limit_bytes=56 * 1024 * 1024
        ),
    )(hsel, tab, pos, wflat, *amp_chunks, m1, m2)


def on_device(amplitudes, integrals, tile_mask, k_irrep, n_irrep, stored_tile):
    slab = lax.axis_index("rep")
    column = lax.axis_index("col")
    n_col = lax.axis_size("col")
    nz = lax.axis_size("z")
    nx = lax.axis_size("x")
    n_row = nz * nx
    zi = lax.axis_index("z")
    xi = lax.axis_index("x")

    ncol = integrals.shape[1]
    tiles_col = ncol // TS
    stored_rows = integrals.shape[0]
    slab_tiles = stored_rows * n_row // TS
    mrow = amplitudes.shape[0]
    chunk_tiles = amplitudes.shape[1] // TS

    n_labels = lax.dynamic_slice_in_dim(n_irrep, column * tiles_col, tiles_col)
    mask_cols = lax.dynamic_slice_in_dim(tile_mask, column * tiles_col, tiles_col, 1)
    slots = lax.dynamic_slice_in_dim(stored_tile, slab * slab_tiles, slab_tiles)
    same = jnp.take(k_irrep, slots)[:, None] == n_labels[None, :]
    occupied = jnp.take(mask_cols, slots, axis=0) == 1
    weights = jnp.logical_and(same, occupied).astype(jnp.int32)
    local_ids = slots - slab * slab_tiles
    inverse = jnp.zeros((slab_tiles,), jnp.int32).at[local_ids].set(
        jnp.arange(slab_tiles, dtype=jnp.int32)
    )
    q = jnp.arange(n_col * chunk_tiles, dtype=jnp.int32)
    tab = jnp.take(inverse, ((column + q // chunk_tiles) % n_col) * chunk_tiles + q % chunk_tiles)

    amp_chunks = ring_gather(amplitudes, "col", n_col, n_col, 1)

    assert stored_rows == TS
    hr = stored_rows // 2
    g1 = lax.all_gather(integrals[:hr], "z", axis=0, tiled=False)
    m1 = jnp.stack(ring_gather(g1, ("z", "x"), n_row, nx, 1)).reshape(n_row * hr, ncol)
    xs = ring_gather(integrals[hr:], ("z", "x"), n_row, nx, 1)
    zs = ring_gather(jnp.stack(xs), ("z", "x"), n_row, nz, nx)
    m2 = jnp.stack(zs).reshape(n_row * hr, ncol)
    sl = jnp.arange(slab_tiles, dtype=jnp.int32)
    pos = jnp.concatenate([((sl % nx - xi) % nx) * nz + sl // nx,
                           ((sl // nx - zi) % nz) * nx + (sl % nx - xi) % nx])

    n_rep = lax.axis_size("rep")
    width = ncol // n_rep
    wflat = weights.reshape(-1)
    other = (1 - slab).astype(jnp.int32).reshape(1)
    own = slab.astype(jnp.int32).reshape(1)
    send = ladder_matmul(other, tab, pos, wflat, amp_chunks, m1, m2, tiles_col, width)
    got = lax.ppermute(send, "rep", [(0, 1), (1, 0)])
    keep = ladder_matmul(own, tab, pos, wflat, amp_chunks, m1, m2, tiles_col, width)
    return (keep + got).astype(jnp.bfloat16)


def solution(mesh):
    nrow = mesh.shape["row"]
    nx = X_RING if nrow % X_RING == 0 else 1
    devices = mesh.devices.reshape(nrow // nx, nx, mesh.shape["col"], mesh.shape["rep"])
    fine = Mesh(devices, ("z", "x", "col", "rep"))
    rows = ("z", "x")
    placed = (P(rows, ("rep", "col")), P(("rep",) + rows, "col"), P(), P(), P(), P())
    return jax.shard_map(
        on_device, mesh=fine, in_specs=placed, out_specs=P(rows, ("col", "rep")), check_vma=False
    )
```

```python
import functools

import jax
import jax.numpy as jnp
from jax import lax
from jax.experimental import pallas as pl
from jax.experimental.pallas import tpu as pltpu
from jax.sharding import Mesh, PartitionSpec as P

TS = 128
X_RING = 4
GROUP = 4
TN = 256
TM = 256


def ring_perm(total, n, stride, step):
    pairs = []
    for i in range(total):
        base = (i // (stride * n)) * (stride * n) + i % stride
        pos = (i // stride) % n
        pairs.append((i, base + ((pos + step) % n) * stride))
    return pairs


class Ring:
    def __init__(self, x, axis, total, n, stride):
        self.axis, self.n = axis, n
        self.plus = ring_perm(total, n, stride, 1)
        self.minus = ring_perm(total, n, stride, -1)
        self.chunks = {0: x}
        self.cur_p, self.cur_m = x, x
        self.k = 0
        self.steps = 0 if n == 1 else (n - 1) // 2 + (1 if n % 2 == 0 else 0)

    def step(self):
        self.k += 1
        k, n = self.k, self.n
        if n == 2:
            self.chunks[1] = lax.ppermute(self.cur_p, self.axis, self.plus)
        elif k <= (n - 1) // 2:
            self.cur_p = lax.ppermute(self.cur_p, self.axis, self.plus)
            self.cur_m = lax.ppermute(self.cur_m, self.axis, self.minus)
            self.chunks[(-k) % n] = self.cur_p
            self.chunks[k] = self.cur_m
        else:
            h = self.cur_p.shape[0] // 2
            first = lax.ppermute(self.cur_p[:h], self.axis, self.plus)
            second = lax.ppermute(self.cur_m[h:], self.axis, self.minus)
            self.chunks[n // 2] = jnp.concatenate([first, second], axis=0)

    def result(self):
        return jnp.stack([self.chunks[d] for d in range(self.n)])


def ladder_kernel(chunk_tiles, tiles_col, hsel_ref, tab_ref, pos_ref, w_ref, *refs):
    n_chunks = len(refs) - 3
    a_refs = refs[:n_chunks]
    m_ref, o_ref, mg_ref = refs[n_chunks:]
    tn = o_ref.shape[1]
    per = tn // TS
    first_tile = hsel_ref[0] * per
    ck = chunk_tiles * TS

    @pl.when(pl.program_id(0) == 0)
    def _():
        col_tile = lax.broadcasted_iota(jnp.int32, (1, tn), 1) // TS
        for q in range(n_chunks * chunk_tiles):
            s = tab_ref[q]
            piece = m_ref[pl.ds(pl.multiple_of(pos_ref[s] * TS, TS), TS), :]
            wv = jnp.zeros((1, tn), jnp.int32)
            for t in range(per):
                wv = jnp.where(col_tile == t, w_ref[s * tiles_col + first_tile + t], wv)
            mg_ref[q * TS:(q + 1) * TS, :] = jnp.where(wv != 0, piece, jnp.zeros_like(piece))

    acc = None
    for k in range(n_chunks):
        term = jnp.dot(a_refs[k][...], mg_ref[k * ck:(k + 1) * ck, :], preferred_element_type=jnp.float32)
        acc = term if acc is None else acc + term
    o_ref[...] = acc


def ladder_matmul(hsel, tab, pos, wflat, amp_chunks, m_all, tiles_col):
    mrow, ck = amp_chunks[0].shape
    n_chunks = len(amp_chunks)
    kk, width = m_all.shape
    tm = min(TM, mrow)
    kernel = functools.partial(ladder_kernel, ck // TS, tiles_col)
    a_spec = pl.BlockSpec((tm, ck), lambda i, h, t, p, w: (i, 0))
    return pl.pallas_call(
        kernel,
        out_shape=jax.ShapeDtypeStruct((mrow, width), jnp.float32),
        grid_spec=pltpu.PrefetchScalarGridSpec(
            num_scalar_prefetch=4,
            grid=(mrow // tm,),
            in_specs=[a_spec] * n_chunks + [pl.BlockSpec((kk, width), lambda i, h, t, p, w: (0, 0))],
            out_specs=pl.BlockSpec((tm, width), lambda i, h, t, p, w: (i, 0)),
            scratch_shapes=[pltpu.VMEM((n_chunks * ck, width), m_all.dtype)],
        ),
        compiler_params=pltpu.CompilerParams(
            dimension_semantics=("arbitrary",), vmem_limit_bytes=56 * 1024 * 1024
        ),
    )(hsel, tab, pos, wflat, *amp_chunks, m_all)


def on_device(amplitudes, integrals, tile_mask, k_irrep, n_irrep, stored_tile):
    slab = lax.axis_index("rep")
    column = lax.axis_index("col")
    n_col = lax.axis_size("col")
    nz = lax.axis_size("z")
    nx = lax.axis_size("x")
    n_row = nz * nx
    zi = lax.axis_index("z")
    xi = lax.axis_index("x")

    ncol = integrals.shape[1]
    tiles_col = ncol // TS
    stored_rows = integrals.shape[0]
    slab_tiles = stored_rows * n_row // TS
    mrow = amplitudes.shape[0]
    chunk_tiles = amplitudes.shape[1] // TS

    n_labels = lax.dynamic_slice_in_dim(n_irrep, column * tiles_col, tiles_col)
    mask_cols = lax.dynamic_slice_in_dim(tile_mask, column * tiles_col, tiles_col, 1)
    slots = lax.dynamic_slice_in_dim(stored_tile, slab * slab_tiles, slab_tiles)
    same = jnp.take(k_irrep, slots)[:, None] == n_labels[None, :]
    occupied = jnp.take(mask_cols, slots, axis=0) == 1
    weights = jnp.logical_and(same, occupied).astype(jnp.int32)
    local_ids = slots - slab * slab_tiles
    inverse = jnp.zeros((slab_tiles,), jnp.int32).at[local_ids].set(
        jnp.arange(slab_tiles, dtype=jnp.int32)
    )
    q = jnp.arange(n_col * chunk_tiles, dtype=jnp.int32)
    tab = jnp.take(inverse, ((column + q // chunk_tiles) % n_col) * chunk_tiles + q % chunk_tiles)

    n_rep = lax.axis_size("rep")
    width = ncol // n_rep
    wflat = weights.reshape(-1)
    other = (1 - slab).astype(jnp.int32).reshape(1)
    own = slab.astype(jnp.int32).reshape(1)
    rows = ("z", "x")

    plus = ring_perm(n_col, n_col, 1, 1)
    minus = ring_perm(n_col, n_col, 1, -1)
    from_left = lax.ppermute(amplitudes, "col", plus)
    from_right = lax.ppermute(amplitudes, "col", minus)

    send_cols = lax.dynamic_slice_in_dim(integrals, other[0] * width, width, 1)
    own_cols = lax.dynamic_slice_in_dim(integrals, own[0] * width, width, 1)
    m_own = lax.all_gather(own_cols, rows, axis=0, tiled=True)
    short = Ring(send_cols, rows, n_row, nx, 1)
    for _ in range(short.steps):
        short.step()
    ring = Ring(short.result(), rows, n_row, nz, nx)
    far = None
    for i in range(ring.steps):
        ring.step()
        if i + 1 == 2:
            ring.cur_p, ring.cur_m, from_left, from_right = lax.optimization_barrier(
                (ring.cur_p, ring.cur_m, from_left, from_right)
            )
            ha = mrow // 2
            far = jnp.concatenate(
                [lax.ppermute(from_left[:ha], "col", plus), lax.ppermute(from_right[ha:], "col", minus)],
                axis=0,
            )
    m_send = ring.result().reshape(n_row * stored_rows, width)
    sl = jnp.arange(slab_tiles, dtype=jnp.int32)
    pos_ring = ((sl // nx - zi) % nz) * nx + (sl % nx - xi) % nx
    chunks = [amplitudes, from_right, far, from_left]

    send = ladder_matmul(other, tab, pos_ring, wflat, chunks, m_send, tiles_col)
    got = lax.ppermute(send, "rep", [(0, 1), (1, 0)])
    keep = ladder_matmul(own, tab, sl, wflat, chunks, m_own, tiles_col)
    return (keep + got).astype(jnp.bfloat16)


def solution(mesh):
    nrow = mesh.shape["row"]
    nx = X_RING if nrow % X_RING == 0 else 1
    devices = mesh.devices.reshape(nrow // nx, nx, mesh.shape["col"], mesh.shape["rep"])
    fine = Mesh(devices, ("z", "x", "col", "rep"))
    rows = ("z", "x")
    placed = (P(rows, ("rep", "col")), P(("rep",) + rows, "col"), P(), P(), P(), P())
    return jax.shard_map(
        on_device, mesh=fine, in_specs=placed, out_specs=P(rows, ("col", "rep")), check_vma=False
    )
```

```python
import functools

import jax
import jax.numpy as jnp
from jax import lax
from jax.experimental import pallas as pl
from jax.experimental.pallas import tpu as pltpu
from jax.sharding import Mesh, PartitionSpec as P

TS = 128
X_RING = 4
GROUP = 4
TN = 256
TM = 256


def ring_perm(total, n, stride, step):
    pairs = []
    for i in range(total):
        base = (i // (stride * n)) * (stride * n) + i % stride
        pos = (i // stride) % n
        pairs.append((i, base + ((pos + step) % n) * stride))
    return pairs


def ring_gather(x, axis, total, n, stride):
    if n == 1:
        return [x]
    plus = ring_perm(total, n, stride, 1)
    minus = ring_perm(total, n, stride, -1)
    chunks = {0: x}
    if n == 2:
        chunks[1] = lax.ppermute(x, axis, plus)
        return [chunks[0], chunks[1]]
    cur_p, cur_m = x, x
    for k in range(1, (n - 1) // 2 + 1):
        cur_p = lax.ppermute(cur_p, axis, plus)
        cur_m = lax.ppermute(cur_m, axis, minus)
        chunks[(-k) % n] = cur_p
        chunks[k] = cur_m
    if n % 2 == 0:
        h = cur_p.shape[0] // 2
        first = lax.ppermute(cur_p[:h], axis, plus)
        second = lax.ppermute(cur_m[h:], axis, minus)
        chunks[n // 2] = jnp.concatenate([first, second], axis=0)
    return [chunks[d] for d in range(n)]


def ladder_kernel(n_chunks, chunk_tiles, tiles_col, nx, hsel_ref, tab_ref, pos_ref, w_ref, *refs):
    a_refs = refs[:n_chunks]
    m1_ref = refs[n_chunks]
    z_refs = refs[n_chunks + 1:-2]
    o_ref, mg_ref = refs[-2:]
    tn = o_ref.shape[1]
    per = tn // TS
    hr = m1_ref.shape[0] // tab_ref.shape[0]
    first_tile = hsel_ref[0] * per
    ck = chunk_tiles * TS

    @pl.when(pl.program_id(0) == 0)
    def _():
        col_tile = lax.broadcasted_iota(jnp.int32, (1, tn), 1) // TS
        for q in range(n_chunks * chunk_tiles):
            s = tab_ref[q]
            ps = pos_ref[s]
            top = m1_ref[pl.ds(pl.multiple_of(s * hr, hr), hr), :]
            wv = jnp.zeros((1, tn), jnp.int32)
            for t in range(per):
                wv = jnp.where(col_tile == t, w_ref[s * tiles_col + first_tile + t], wv)
            keep = wv != 0
            mg_ref[q * TS:q * TS + hr, :] = jnp.where(keep, top, jnp.zeros_like(top))
            dz = ps // nx
            dx = ps % nx
            for b in range(len(z_refs)):
                @pl.when(dz == b)
                def _():
                    bottom = z_refs[b][pl.ds(pl.multiple_of(dx * hr, hr), hr), :]
                    mg_ref[q * TS + hr:(q + 1) * TS, :] = jnp.where(keep, bottom, jnp.zeros_like(bottom))

    acc = None
    for k in range(n_chunks):
        term = jnp.dot(a_refs[k][...], mg_ref[k * ck:(k + 1) * ck, :], preferred_element_type=jnp.float32)
        acc = term if acc is None else acc + term
    o_ref[...] = acc


def ladder_matmul(hsel, tab, pos, wflat, amp_chunks, m1, z_pieces, tiles_col, width, nx):
    mrow, ck = amp_chunks[0].shape
    n_chunks = len(amp_chunks)
    kk, ncol = m1.shape
    tm = min(TM, mrow)
    kernel = functools.partial(ladder_kernel, n_chunks, ck // TS, tiles_col, nx)
    m_spec = pl.BlockSpec((kk, width), lambda i, h, t, p, w: (0, h[0]))
    z_spec = pl.BlockSpec((z_pieces[0].shape[0], width), lambda i, h, t, p, w: (0, h[0]))
    a_spec = pl.BlockSpec((tm, ck), lambda i, h, t, p, w: (i, 0))
    return pl.pallas_call(
        kernel,
        out_shape=jax.ShapeDtypeStruct((mrow, width), jnp.float32),
        grid_spec=pltpu.PrefetchScalarGridSpec(
            num_scalar_prefetch=4,
            grid=(mrow // tm,),
            in_specs=[a_spec] * n_chunks + [m_spec] + [z_spec] * len(z_pieces),
            out_specs=pl.BlockSpec((tm, width), lambda i, h, t, p, w: (i, 0)),
            scratch_shapes=[pltpu.VMEM((n_chunks * ck, width), m1.dtype)],
        ),
        compiler_params=pltpu.CompilerParams(
            dimension_semantics=("arbitrary",), vmem_limit_bytes=56 * 1024 * 1024
        ),
    )(hsel, tab, pos, wflat, *amp_chunks, m1, *z_pieces)


def on_device(amplitudes, integrals, tile_mask, k_irrep, n_irrep, stored_tile):
    slab = lax.axis_index("rep")
    column = lax.axis_index("col")
    n_col = lax.axis_size("col")
    nz = lax.axis_size("z")
    nx = lax.axis_size("x")
    n_row = nz * nx
    zi = lax.axis_index("z")
    xi = lax.axis_index("x")

    ncol = integrals.shape[1]
    tiles_col = ncol // TS
    stored_rows = integrals.shape[0]
    slab_tiles = stored_rows * n_row // TS
    mrow = amplitudes.shape[0]
    chunk_tiles = amplitudes.shape[1] // TS

    n_labels = lax.dynamic_slice_in_dim(n_irrep, column * tiles_col, tiles_col)
    mask_cols = lax.dynamic_slice_in_dim(tile_mask, column * tiles_col, tiles_col, 1)
    slots = lax.dynamic_slice_in_dim(stored_tile, slab * slab_tiles, slab_tiles)
    same = jnp.take(k_irrep, slots)[:, None] == n_labels[None, :]
    occupied = jnp.take(mask_cols, slots, axis=0) == 1
    weights = jnp.logical_and(same, occupied).astype(jnp.int32)
    local_ids = slots - slab * slab_tiles
    inverse = jnp.zeros((slab_tiles,), jnp.int32).at[local_ids].set(
        jnp.arange(slab_tiles, dtype=jnp.int32)
    )
    q = jnp.arange(n_col * chunk_tiles, dtype=jnp.int32)
    tab = jnp.take(inverse, ((column + q // chunk_tiles) % n_col) * chunk_tiles + q % chunk_tiles)

    amp_chunks = ring_gather(amplitudes, "col", n_col, n_col, 1)

    assert stored_rows == TS
    hr = stored_rows // 2
    m1 = lax.all_gather(integrals[:hr], ("z", "x"), axis=0, tiled=True)
    xs = ring_gather(integrals[hr:], ("z", "x"), n_row, nx, 1)
    zs = ring_gather(jnp.stack(xs), ("z", "x"), n_row, nz, nx)
    z_pieces = [z.reshape(nx * hr, ncol) for z in zs]
    sl = jnp.arange(slab_tiles, dtype=jnp.int32)
    pos = ((sl // nx - zi) % nz) * nx + (sl % nx - xi) % nx

    n_rep = lax.axis_size("rep")
    width = ncol // n_rep
    wflat = weights.reshape(-1)
    other = (1 - slab).astype(jnp.int32).reshape(1)
    own = slab.astype(jnp.int32).reshape(1)
    send = ladder_matmul(other, tab, pos, wflat, amp_chunks, m1, z_pieces, tiles_col, width, nx)
    got = lax.ppermute(send, "rep", [(0, 1), (1, 0)])
    keep = ladder_matmul(own, tab, pos, wflat, amp_chunks, m1, z_pieces, tiles_col, width, nx)
    return (keep + got).astype(jnp.bfloat16)


def solution(mesh):
    nrow = mesh.shape["row"]
    nx = X_RING if nrow % X_RING == 0 else 1
    devices = mesh.devices.reshape(nrow // nx, nx, mesh.shape["col"], mesh.shape["rep"])
    fine = Mesh(devices, ("z", "x", "col", "rep"))
    rows = ("z", "x")
    placed = (P(rows, ("rep", "col")), P(("rep",) + rows, "col"), P(), P(), P(), P())
    return jax.shard_map(
        on_device, mesh=fine, in_specs=placed, out_specs=P(rows, ("col", "rep")), check_vma=False
    )
```

```python
import functools

import jax
import jax.numpy as jnp
from jax import lax
from jax.experimental import pallas as pl
from jax.experimental.pallas import tpu as pltpu
from jax.sharding import Mesh, PartitionSpec as P

TS = 128
X_RING = 4
GROUP = 4
TN = 256


def ring_perm(total, n, stride, step):
    pairs = []
    for i in range(total):
        base = (i // (stride * n)) * (stride * n) + i % stride
        pos = (i // stride) % n
        pairs.append((i, base + ((pos + step) % n) * stride))
    return pairs


def ring_gather(x, axis, total, n, stride):
    if n == 1:
        return [x]
    plus = ring_perm(total, n, stride, 1)
    minus = ring_perm(total, n, stride, -1)
    chunks = {0: x}
    if n == 2:
        chunks[1] = lax.ppermute(x, axis, plus)
        return [chunks[0], chunks[1]]
    cur_p, cur_m = x, x
    for k in range(1, (n - 1) // 2 + 1):
        cur_p = lax.ppermute(cur_p, axis, plus)
        cur_m = lax.ppermute(cur_m, axis, minus)
        chunks[(-k) % n] = cur_p
        chunks[k] = cur_m
    if n % 2 == 0:
        h = cur_p.shape[0] // 2
        first = lax.ppermute(cur_p[:h], axis, plus)
        second = lax.ppermute(cur_m[h:], axis, minus)
        chunks[n // 2] = jnp.concatenate([first, second], axis=0)
    return [chunks[d] for d in range(n)]


class Ring:
    def __init__(self, x, axis, total, n, stride):
        self.axis, self.n = axis, n
        self.plus = ring_perm(total, n, stride, 1)
        self.minus = ring_perm(total, n, stride, -1)
        self.chunks = {0: x}
        self.cur_p, self.cur_m = x, x
        self.k = 0
        self.steps = 0 if n == 1 else (n - 1) // 2 + (1 if n % 2 == 0 else 0)

    def step(self):
        self.k += 1
        k, n = self.k, self.n
        if n == 2:
            self.chunks[1] = lax.ppermute(self.cur_p, self.axis, self.plus)
        elif k <= (n - 1) // 2:
            self.cur_p = lax.ppermute(self.cur_p, self.axis, self.plus)
            self.cur_m = lax.ppermute(self.cur_m, self.axis, self.minus)
            self.chunks[(-k) % n] = self.cur_p
            self.chunks[k] = self.cur_m
        else:
            h = self.cur_p.shape[0] // 2
            first = lax.ppermute(self.cur_p[:h], self.axis, self.plus)
            second = lax.ppermute(self.cur_m[h:], self.axis, self.minus)
            self.chunks[n // 2] = jnp.concatenate([first, second], axis=0)

    def result(self):
        return jnp.stack([self.chunks[d] for d in range(self.n)])


def ladder_kernel(n_chunks, chunk_tiles, tiles_col, bpw, hsel_ref, tab_ref, pos_ref, w_ref, *refs):
    a_refs = refs[:n_chunks]
    m1_ref, m2_ref, o_ref = refs[n_chunks:n_chunks + 3]
    j = pl.program_id(0)
    tn = o_ref.shape[1]
    per = tn // TS
    hr = m1_ref.shape[0] // tab_ref.shape[0]
    first_tile = (hsel_ref[0] * bpw + j) * per
    col_tile = lax.broadcasted_iota(jnp.int32, (1, tn), 1) // TS
    groups_per_chunk = chunk_tiles // GROUP
    for g in range(n_chunks * groups_per_chunk):
        d = g // groups_per_chunk
        off = (g % groups_per_chunk) * GROUP * TS
        pieces = []
        for u in range(GROUP):
            s = tab_ref[g * GROUP + u]
            ps = pos_ref[s]
            top = m1_ref[pl.ds(pl.multiple_of(s * hr, hr), hr), :]
            bottom = m2_ref[pl.ds(pl.multiple_of(ps * hr, hr), hr), :]
            piece = jnp.concatenate([top, bottom], axis=0)
            wv = jnp.zeros((1, tn), jnp.int32)
            for t in range(per):
                wv = jnp.where(col_tile == t, w_ref[s * tiles_col + first_tile + t], wv)
            pieces.append(jnp.where(wv != 0, piece, jnp.zeros_like(piece)))
        mg = jnp.concatenate(pieces, axis=0)
        term = jnp.dot(a_refs[d][:, off:off + GROUP * TS], mg, preferred_element_type=jnp.float32)
        if g == 0:
            o_ref[...] = term
        else:
            o_ref[...] += term


def ladder_matmul(hsel, tab, pos, wflat, amp_chunks, m1, m2, tiles_col, width):
    mrow, ck = amp_chunks[0].shape
    n_chunks = len(amp_chunks)
    kk, ncol = m1.shape
    tn = min(TN, width)
    bpw = width // tn
    kernel = functools.partial(ladder_kernel, n_chunks, ck // TS, tiles_col, bpw)
    a_spec = pl.BlockSpec((mrow, ck), lambda j, h, t, p, w: (0, 0))
    m_spec = pl.BlockSpec((kk, tn), lambda j, h, t, p, w: (0, h[0] * bpw + j))
    return pl.pallas_call(
        kernel,
        out_shape=jax.ShapeDtypeStruct((mrow, width), jnp.float32),
        grid_spec=pltpu.PrefetchScalarGridSpec(
            num_scalar_prefetch=4,
            grid=(bpw,),
            in_specs=[a_spec] * n_chunks + [m_spec, m_spec],
            out_specs=pl.BlockSpec((mrow, tn), lambda j, h, t, p, w: (0, j)),
        ),
        compiler_params=pltpu.CompilerParams(
            dimension_semantics=("arbitrary",), vmem_limit_bytes=56 * 1024 * 1024
        ),
    )(hsel, tab, pos, wflat, *amp_chunks, m1, m2)


def on_device(amplitudes, integrals, tile_mask, k_irrep, n_irrep, stored_tile):
    slab = lax.axis_index("rep")
    column = lax.axis_index("col")
    n_col = lax.axis_size("col")
    nz = lax.axis_size("z")
    nx = lax.axis_size("x")
    n_row = nz * nx
    zi = lax.axis_index("z")
    xi = lax.axis_index("x")

    ncol = integrals.shape[1]
    tiles_col = ncol // TS
    stored_rows = integrals.shape[0]
    slab_tiles = stored_rows * n_row // TS
    mrow = amplitudes.shape[0]
    chunk_tiles = amplitudes.shape[1] // TS

    n_labels = lax.dynamic_slice_in_dim(n_irrep, column * tiles_col, tiles_col)
    mask_cols = lax.dynamic_slice_in_dim(tile_mask, column * tiles_col, tiles_col, 1)
    slots = lax.dynamic_slice_in_dim(stored_tile, slab * slab_tiles, slab_tiles)
    same = jnp.take(k_irrep, slots)[:, None] == n_labels[None, :]
    occupied = jnp.take(mask_cols, slots, axis=0) == 1
    weights = jnp.logical_and(same, occupied).astype(jnp.int32)
    local_ids = slots - slab * slab_tiles
    inverse = jnp.zeros((slab_tiles,), jnp.int32).at[local_ids].set(
        jnp.arange(slab_tiles, dtype=jnp.int32)
    )
    q = jnp.arange(n_col * chunk_tiles, dtype=jnp.int32)
    tab = jnp.take(inverse, ((column + q // chunk_tiles) % n_col) * chunk_tiles + q % chunk_tiles)

    plus = ring_perm(n_col, n_col, 1, 1)
    minus = ring_perm(n_col, n_col, 1, -1)
    from_left = lax.ppermute(amplitudes, "col", plus)
    from_right = lax.ppermute(amplitudes, "col", minus)

    assert stored_rows == TS
    hr = stored_rows // 2
    m1 = lax.all_gather(integrals[:hr], ("z", "x"), axis=0, tiled=True)
    xs = ring_gather(integrals[hr:], ("z", "x"), n_row, nx, 1)
    ring = Ring(jnp.stack(xs), ("z", "x"), n_row, nz, nx)
    far = None
    for i in range(ring.steps):
        ring.step()
        if i + 1 == 2:
            ring.cur_p, ring.cur_m, from_left, from_right = lax.optimization_barrier(
                (ring.cur_p, ring.cur_m, from_left, from_right)
            )
            ha = mrow // 2
            far = jnp.concatenate(
                [lax.ppermute(from_left[:ha], "col", plus), lax.ppermute(from_right[ha:], "col", minus)],
                axis=0,
            )
        if i + 1 == 3:
            ring.cur_p, ring.cur_m, far = lax.optimization_barrier((ring.cur_p, ring.cur_m, far))
    amp_chunks = [amplitudes, from_right, far, from_left]
    zs = [ring.chunks[d] for d in range(nz)]
    m2 = jnp.stack(zs).reshape(n_row * hr, ncol)
    sl = jnp.arange(slab_tiles, dtype=jnp.int32)
    pos = ((sl // nx - zi) % nz) * nx + (sl % nx - xi) % nx

    n_rep = lax.axis_size("rep")
    width = ncol // n_rep
    wflat = weights.reshape(-1)
    other = (1 - slab).astype(jnp.int32).reshape(1)
    own = slab.astype(jnp.int32).reshape(1)
    send = ladder_matmul(other, tab, pos, wflat, amp_chunks, m1, m2, tiles_col, width)
    got = lax.ppermute(send, "rep", [(0, 1), (1, 0)])
    keep = ladder_matmul(own, tab, pos, wflat, amp_chunks, m1, m2, tiles_col, width)
    return (keep + got).astype(jnp.bfloat16)


def solution(mesh):
    nrow = mesh.shape["row"]
    nx = X_RING if nrow % X_RING == 0 else 1
    devices = mesh.devices.reshape(nrow // nx, nx, mesh.shape["col"], mesh.shape["rep"])
    fine = Mesh(devices, ("z", "x", "col", "rep"))
    rows = ("z", "x")
    placed = (P(rows, ("rep", "col")), P(("rep",) + rows, "col"), P(), P(), P(), P())
    return jax.shard_map(
        on_device, mesh=fine, in_specs=placed, out_specs=P(rows, ("col", "rep")), check_vma=False
    )
```

```python
import functools

import jax
import jax.numpy as jnp
from jax import lax
from jax.experimental import pallas as pl
from jax.experimental.pallas import tpu as pltpu
from jax.sharding import Mesh, PartitionSpec as P

TS = 128
X_RING = 4
GROUP = 4
TN = 256


def ring_perm(total, n, stride, step):
    pairs = []
    for i in range(total):
        base = (i // (stride * n)) * (stride * n) + i % stride
        pos = (i // stride) % n
        pairs.append((i, base + ((pos + step) % n) * stride))
    return pairs


def ring_gather(x, axis, total, n, stride):
    if n == 1:
        return [x]
    plus = ring_perm(total, n, stride, 1)
    minus = ring_perm(total, n, stride, -1)
    chunks = {0: x}
    if n == 2:
        chunks[1] = lax.ppermute(x, axis, plus)
        return [chunks[0], chunks[1]]
    cur_p, cur_m = x, x
    for k in range(1, (n - 1) // 2 + 1):
        cur_p = lax.ppermute(cur_p, axis, plus)
        cur_m = lax.ppermute(cur_m, axis, minus)
        chunks[(-k) % n] = cur_p
        chunks[k] = cur_m
    if n % 2 == 0:
        h = cur_p.shape[0] // 2
        first = lax.ppermute(cur_p[:h], axis, plus)
        second = lax.ppermute(cur_m[h:], axis, minus)
        chunks[n // 2] = jnp.concatenate([first, second], axis=0)
    return [chunks[d] for d in range(n)]


def ladder_kernel(n_chunks, chunk_tiles, tiles_col, bpw, hsel_ref, tab_ref, pos_ref, w_ref, *refs):
    a_refs = refs[:n_chunks]
    m1_ref, m2_ref, o_ref = refs[n_chunks:n_chunks + 3]
    j = pl.program_id(0)
    tn = o_ref.shape[1]
    per = tn // TS
    hr = m1_ref.shape[0] // tab_ref.shape[0]
    hr2 = m2_ref.shape[0] // tab_ref.shape[0]
    first_tile = (hsel_ref[0] * bpw + j) * per
    col_tile = lax.broadcasted_iota(jnp.int32, (1, tn), 1) // TS
    groups_per_chunk = chunk_tiles // GROUP
    for g in range(n_chunks * groups_per_chunk):
        d = g // groups_per_chunk
        off = (g % groups_per_chunk) * GROUP * TS
        pieces = []
        for u in range(GROUP):
            s = tab_ref[g * GROUP + u]
            ps = pos_ref[s]
            top = m1_ref[pl.ds(pl.multiple_of(s * hr, hr), hr), :]
            bottom = m2_ref[pl.ds(pl.multiple_of(ps * hr2, hr2), hr2), :]
            piece = jnp.concatenate([top, bottom], axis=0)
            wv = jnp.zeros((1, tn), jnp.int32)
            for t in range(per):
                wv = jnp.where(col_tile == t, w_ref[s * tiles_col + first_tile + t], wv)
            pieces.append(jnp.where(wv != 0, piece, jnp.zeros_like(piece)))
        mg = jnp.concatenate(pieces, axis=0)
        term = jnp.dot(a_refs[d][:, off:off + GROUP * TS], mg, preferred_element_type=jnp.float32)
        if g == 0:
            o_ref[...] = term
        else:
            o_ref[...] += term


def ladder_matmul(hsel, tab, pos, wflat, amp_chunks, m1, m2, tiles_col, width):
    mrow, ck = amp_chunks[0].shape
    n_chunks = len(amp_chunks)
    kk, ncol = m1.shape
    tn = min(TN, width)
    bpw = width // tn
    kernel = functools.partial(ladder_kernel, n_chunks, ck // TS, tiles_col, bpw)
    a_spec = pl.BlockSpec((mrow, ck), lambda j, h, t, p, w: (0, 0))
    m_spec = pl.BlockSpec((kk, tn), lambda j, h, t, p, w: (0, h[0] * bpw + j))
    return pl.pallas_call(
        kernel,
        out_shape=jax.ShapeDtypeStruct((mrow, width), jnp.float32),
        grid_spec=pltpu.PrefetchScalarGridSpec(
            num_scalar_prefetch=4,
            grid=(bpw,),
            in_specs=[a_spec] * n_chunks + [m_spec, pl.BlockSpec((m2.shape[0], tn), lambda j, h, t, p, w: (0, h[0] * bpw + j))],
            out_specs=pl.BlockSpec((mrow, tn), lambda j, h, t, p, w: (0, j)),
        ),
        compiler_params=pltpu.CompilerParams(
            dimension_semantics=("arbitrary",), vmem_limit_bytes=56 * 1024 * 1024
        ),
    )(hsel, tab, pos, wflat, *amp_chunks, m1, m2)


def on_device(amplitudes, integrals, tile_mask, k_irrep, n_irrep, stored_tile):
    slab = lax.axis_index("rep")
    column = lax.axis_index("col")
    n_col = lax.axis_size("col")
    nz = lax.axis_size("z")
    nx = lax.axis_size("x")
    n_row = nz * nx
    zi = lax.axis_index("z")
    xi = lax.axis_index("x")

    ncol = integrals.shape[1]
    tiles_col = ncol // TS
    stored_rows = integrals.shape[0]
    slab_tiles = stored_rows * n_row // TS
    mrow = amplitudes.shape[0]
    chunk_tiles = amplitudes.shape[1] // TS

    n_labels = lax.dynamic_slice_in_dim(n_irrep, column * tiles_col, tiles_col)
    mask_cols = lax.dynamic_slice_in_dim(tile_mask, column * tiles_col, tiles_col, 1)
    slots = lax.dynamic_slice_in_dim(stored_tile, slab * slab_tiles, slab_tiles)
    same = jnp.take(k_irrep, slots)[:, None] == n_labels[None, :]
    occupied = jnp.take(mask_cols, slots, axis=0) == 1
    weights = jnp.logical_and(same, occupied).astype(jnp.int32)
    local_ids = slots - slab * slab_tiles
    inverse = jnp.zeros((slab_tiles,), jnp.int32).at[local_ids].set(
        jnp.arange(slab_tiles, dtype=jnp.int32)
    )
    q = jnp.arange(n_col * chunk_tiles, dtype=jnp.int32)
    tab = jnp.take(inverse, ((column + q // chunk_tiles) % n_col) * chunk_tiles + q % chunk_tiles)

    amp_chunks = ring_gather(amplitudes, "col", n_col, n_col, 1)

    assert stored_rows == TS
    hr = stored_rows * 3 // 4
    m1 = lax.all_gather(integrals[:hr], ("z", "x"), axis=0, tiled=True)
    xs = ring_gather(integrals[hr:], ("z", "x"), n_row, nx, 1)
    zs = ring_gather(jnp.stack(xs), ("z", "x"), n_row, nz, nx)
    m2 = jnp.stack(zs).reshape(n_row * (stored_rows - hr), ncol)
    sl = jnp.arange(slab_tiles, dtype=jnp.int32)
    pos = ((sl // nx - zi) % nz) * nx + (sl % nx - xi) % nx

    n_rep = lax.axis_size("rep")
    width = ncol // n_rep
    wflat = weights.reshape(-1)
    other = (1 - slab).astype(jnp.int32).reshape(1)
    own = slab.astype(jnp.int32).reshape(1)
    send = ladder_matmul(other, tab, pos, wflat, amp_chunks, m1, m2, tiles_col, width)
    got = lax.ppermute(send, "rep", [(0, 1), (1, 0)])
    keep = ladder_matmul(own, tab, pos, wflat, amp_chunks, m1, m2, tiles_col, width)
    return (keep + got).astype(jnp.bfloat16)


def solution(mesh):
    nrow = mesh.shape["row"]
    nx = X_RING if nrow % X_RING == 0 else 1
    devices = mesh.devices.reshape(nrow // nx, nx, mesh.shape["col"], mesh.shape["rep"])
    fine = Mesh(devices, ("z", "x", "col", "rep"))
    rows = ("z", "x")
    placed = (P(rows, ("rep", "col")), P(("rep",) + rows, "col"), P(), P(), P(), P())
    return jax.shard_map(
        on_device, mesh=fine, in_specs=placed, out_specs=P(rows, ("col", "rep")), check_vma=False
    )
```
